32 devices in a mesh: gx: 4 (over y, x), gy: 8 (over z, core).
Axes of the slice: x: 2, y: 2, z: 4, core: 2. Of those that a mesh axis runs over, the one named last changes fastest.
Arguments:
- fields: float32 [3, 128, 1024], P(None, 'gx', 'gy'), may hold values from -10 to 10
- lift_weight: float32 [12, 64], replicated, may hold values from -1.75 to 1.75
- lift_bias: float32 [64], replicated, may hold values from -3 to 3
- spectral_weight: float32 [2, 8, 8, 64, 64], replicated, may hold values from -4 to 4
- bypass_weight: float32 [64, 64], replicated, may hold values from -0.75 to 0.75
- layer_bias: float32 [64], replicated, may hold values from -3 to 3
- mlp_in_weight: float32 [64, 128], replicated, may hold values from -0.75 to 0.75
- mlp_in_bias: float32 [128], replicated, may hold values from -3 to 3
- mlp_out_weight: float32 [128, 64], replicated, may hold values from -0.5 to 0.5
- mlp_out_bias: float32 [64], replicated, may hold values from -3 to 3
- project_weight: float32 [64, 3], replicated, may hold values from -0.75 to 0.75
- project_bias: float32 [3], replicated, may hold values from -3 to 3
Outputs:
- next_fields: float32 [3, 128, 1024], P(None, 'gx', 'gy')
The draws below stay inside these ranges and needn't reach their ends.
All inputs are finite; a program needn't handle non-finite values.
Results may differ from the reference program's by a relative error of at most 0.0001.
Values sent between devices are 32-bit elements; how exact they have to be, the bound alone decides.
A program may use at most 64 MiB of HBM per device.

```python
import math
import jax
import jax.numpy as jnp
from jax import lax

CX = 32
CY = 128
IN_CHANNELS = 3
C = 64
HID = 128
MODES_X = 8
MODES_Y = 8
STEPS = 2
LIFT_IN = 12
NX = 128
NY = 1024
N_GX = 4
N_GY = 8


def draw_fields(key, part):
    base = jax.random.fold_in(key, 17)
    rough_key, wave_key, column_key, phase_key, amplitude_key = jax.random.split(base, 5)
    terms = 6
    rows = jnp.arange(NX, dtype=jnp.int32)
    cols = jnp.arange(NY, dtype=jnp.int32)
    row_waves = jax.random.randint(wave_key, (IN_CHANNELS, terms), 1, 5)
    col_waves = jax.random.randint(column_key, (IN_CHANNELS, terms), -4, 5)
    phases = jax.random.uniform(phase_key, (IN_CHANNELS, terms), jnp.float32, 0.0, 2.0 * math.pi)
    amplitudes = jax.random.uniform(amplitude_key, (IN_CHANNELS, terms), jnp.float32, 0.4, 0.8)
    smooth = jnp.zeros((IN_CHANNELS, NX, NY), jnp.float32)
    for term in range(terms):
        row_phase = (row_waves[:, term][:, None] * rows[None, :] % NX).astype(jnp.float32) * (2.0 * math.pi / NX)
        col_phase = (col_waves[:, term][:, None] * cols[None, :] % NY).astype(jnp.float32) * (2.0 * math.pi / NY)
        smooth = smooth + amplitudes[:, term, None, None] * jnp.sin(row_phase[:, :, None] + col_phase[:, None, :] + phases[:, term, None, None])
    rough = jax.random.truncated_normal(rough_key, -4.0, 4.0, (IN_CHANNELS, NX, NY), jnp.float32)
    return rough + smooth


def scatter_about(key, dims, deviation, most, held_as=jnp.bfloat16):
    result = deviation * jax.random.normal(key, dims, jnp.float32)
    return jnp.clip(result, min=-most, max=most).astype(held_as)


def setup_inputs(seed: int = 0) -> dict:
    seeds = jax.random.split(jax.random.key(seed), 13)
    return {
        "fields": draw_fields(jax.random.fold_in(seeds[12], 71), 0),
        "lift_weight": scatter_about(seeds[1], (LIFT_IN, C), LIFT_IN ** -0.5, 1.75, jnp.float32),
        "lift_bias": scatter_about(seeds[2], (C,), 0.5, 3.0, jnp.float32),
        "spectral_weight": scatter_about(seeds[3], (2, MODES_X, MODES_Y, C, C), (0.0055 * (CX * CY) ** 0.5), 4.0, jnp.float32),
        "bypass_weight": scatter_about(seeds[4], (C, C), C ** -0.5, 0.75, jnp.float32),
        "layer_bias": scatter_about(seeds[5], (C,), 0.5, 3.0, jnp.float32),
        "mlp_in_weight": scatter_about(seeds[6], (C, HID), C ** -0.5, 0.75, jnp.float32),
        "mlp_in_bias": scatter_about(seeds[7], (HID,), 0.5, 3.0, jnp.float32),
        "mlp_out_weight": scatter_about(seeds[8], (HID, C), HID ** -0.5, 0.5, jnp.float32),
        "mlp_out_bias": scatter_about(seeds[9], (C,), 0.5, 3.0, jnp.float32),
        "project_weight": scatter_about(seeds[10], (C, IN_CHANNELS), C ** -0.5, 0.75, jnp.float32),
        "project_bias": scatter_about(seeds[11], (IN_CHANNELS,), 0.5, 3.0, jnp.float32),
    }


HIGHEST_PRECISION = lax.Precision.HIGHEST


def pointwise(weights, inputs, biases):
    return jnp.einsum("io,ixy->oxy", weights, inputs, precision=HIGHEST_PRECISION) + biases[:, None, None]


def context_window(extent, tile_length, factor):
    positions = jnp.arange(extent, dtype=jnp.int32)
    anchor = (positions // tile_length) * (tile_length // factor) - (factor - 1) * (tile_length // (2 * factor))
    return ((anchor + positions % tile_length) % (extent // factor)).astype(jnp.int32)


def all_contexts(current):
    channels = current.shape[0]
    results = []
    for level_number in (1, 2, 3):
        factor = 2 ** level_number
        pooled = current.reshape(channels, NX // factor, factor, NY // factor, factor).mean(axis=(2, 4))
        rows_window = context_window(NX, CX, factor)
        cols_window = context_window(NY, CY, factor)
        results.append(jnp.take(jnp.take(pooled, rows_window, axis=1), cols_window, axis=2))
    return results


def spectral_tiles(hidden_tiles, spectral_weight):
    tile_rows = hidden_tiles.shape[2]
    tile_cols = hidden_tiles.shape[3]
    spectrum = jnp.fft.rfft2(hidden_tiles, axes=(2, 3))
    ordinal = jnp.arange(MODES_X, dtype=jnp.int32)
    rows_index = jnp.where(ordinal < MODES_X // 2, ordinal, ordinal + tile_rows - MODES_X)
    kept = spectrum[:, :, rows_index, :MODES_Y]
    complex_weight = spectral_weight[0] + 1j * spectral_weight[1]
    mixed_modes = jnp.einsum("gckj,kjco->gokj", kept, complex_weight, precision=HIGHEST_PRECISION)
    full_spectrum = jnp.zeros(spectrum.shape, spectrum.dtype).at[:, :, rows_index, :MODES_Y].set(mixed_modes)
    return jnp.fft.irfft2(full_spectrum, s=(tile_rows, tile_cols), axes=(2, 3))


def reference(fields, lift_weight, lift_bias, spectral_weight, bypass_weight, layer_bias, mlp_in_weight, mlp_in_bias, mlp_out_weight, mlp_out_bias, project_weight, project_bias):
    channels = fields.shape[0]
    hidden_width = lift_weight.shape[1]

    def slab_step(slab):
        hidden = pointwise(lift_weight, slab, lift_bias)
        tiles = hidden.reshape(hidden_width, CX, N_GY, CY).transpose(2, 0, 1, 3)
        spectral = spectral_tiles(tiles, spectral_weight).transpose(1, 2, 0, 3).reshape(hidden_width, CX, NY)
        mixed = jax.nn.gelu(spectral + pointwise(bypass_weight, hidden, layer_bias))
        inner = jax.nn.gelu(pointwise(mlp_in_weight, mixed, mlp_in_bias))
        refined = mixed + pointwise(mlp_out_weight, inner, mlp_out_bias)
        return slab[:channels] + pointwise(project_weight, refined, project_bias)

    current = fields
    for rollout in range(STEPS):
        features = jnp.concatenate([current] + all_contexts(current), axis=0)
        slabs = features.reshape(features.shape[0], N_GX, CX, NY).transpose(1, 0, 2, 3)
        updated = lax.map(slab_step, slabs)
        current = updated.transpose(1, 0, 2, 3).reshape(channels, NX, NY)
    return current
```

```python
import functools
import math

import jax
import jax.numpy as jnp
import numpy as np
from jax import lax
from jax.experimental import pallas as pl
from jax.experimental.pallas import tpu as pltpu
from jax.sharding import PartitionSpec as P

MODES_X = 8
MODES_Y = 8
STEPS = 2
LEVELS = (1, 2, 3)
F32 = jnp.float32
BF16 = jnp.bfloat16
FP = 16
MESH = pl.DeviceIdType.MESH


def np_split(a):
    a = np.asarray(a, np.float32)
    hi = a.astype(jnp.bfloat16)
    lo = (a - hi.astype(np.float32)).astype(jnp.bfloat16)
    return hi, lo


def split(x):
    hi = x.astype(BF16)
    lo = (x - hi.astype(F32)).astype(BF16)
    return hi, lo


def bdot(a, b):
    return jnp.dot(a, b, preferred_element_type=F32)


def ntdot(a, b):
    return lax.dot_general(a, b, (((1,), (1,)), ((), ())), preferred_element_type=F32)


def round_up(n, m):
    return -(-n // m) * m


class Plan:
    def __init__(self, ch, rows, cols, nx, ny):
        self.ch, self.rows, self.cols, self.nx, self.ny = ch, rows, cols, nx, ny
        self.lv = []
        for k in LEVELS:
            p = 2**k
            h = 2 if k == 1 else 1
            nr, nc = rows // p, cols // p
            ur, uc = nr // h, nc // h
            nb = cols // uc
            nq = -(-ch * ur // nb)
            slot_rows = nq if nq in (1, 2, 4) else round_up(nq, 8)
            r0, c0 = -(p - 1) * nr // 2, -(p - 1) * nc // 2
            dxs = sorted({d % (h * nx) for d in range(r0 // ur, (r0 + rows - 1) // ur + 1)})
            dys = sorted({d % (h * ny) for d in range(c0 // uc, (c0 + cols - 1) // uc + 1)})
            slots = [(a, b) for a in dxs for b in dys if (a // h, b // h) != (0, 0)]
            kpad = round_up(len(dxs) * slot_rows, 16)
            self.lv.append(
                dict(p=p, h=h, ur=ur, uc=uc, nb=nb, nq=nq, sr=slot_rows, r0=r0, c0=c0, dxs=dxs, dys=dys,
                     slots=slots, index={q: n for n, q in enumerate(slots)}, kpad=kpad,
                     qrows=round_up(nq, 8))
            )
        def far(m):
            h = self.lv[m[0]]["h"]
            da, db = (m[2] // h) % nx, (m[3] // h) % ny
            return min(da, nx - da) + min(db, ny - db)

        self.messages = sorted(
            ((n, slot, a, b) for n, lv in enumerate(self.lv) for slot, (a, b) in enumerate(lv["slots"])),
            key=lambda m: m[0])
        offs = {(a // lv["h"], b // lv["h"]) for lv in self.lv for a, b in lv["slots"]}
        self.everyone = sorted(offs | {((-a) % nx, (-b) % ny) for a, b in offs})

    def constants(self):
        ch, rows, cols = self.ch, self.rows, self.cols
        q_parts, p_parts, a_parts, place_parts = [], [], [], []
        for lv in self.lv:
            p, h, ur, uc, nb, nq, qr = (lv[x] for x in ("p", "h", "ur", "uc", "nb", "nq", "qrows"))
            q = np.zeros((h, nb, qr, rows * 8), np.float32)
            for hx in range(h):
                for b in range(nb):
                    for t in range(nq):
                        rho = b * nq + t
                        if rho < ch * ur:
                            c, rr = divmod(rho, ur)
                            for u in range(p):
                                q[hx, b, t, ((hx * ur + rr) * p + u) * 8 + c] = 1.0 / p
            q_parts.append(q.reshape(h * nb * qr, rows * 8))
            for hy in range(h):
                pm = np.zeros((cols, cols), np.float32)
                for j in range(uc):
                    for b in range(nb):
                        pm[(hy * uc + j) * p:(hy * uc + j + 1) * p, b * uc + j] = 1.0 / p
                p_parts.append(pm)
            a = np.zeros((ch * rows, lv["kpad"]), np.float32)
            for c in range(ch):
                for w in range(rows):
                    d, rr = divmod(w + lv["r0"], ur)
                    t = (c * ur + rr) % nq
                    a[c * rows + w, lv["dxs"].index(d % (h * self.nx)) * lv["sr"] + t] = 1.0
            a_parts.append(a)
            pl_m = np.zeros((len(lv["dys"]) * cols, cols), np.float32)
            for l in range(cols):
                d, sc = divmod(l + lv["c0"], uc)
                y = lv["dys"].index(d % (h * self.ny))
                for b in range(nb):
                    pl_m[y * cols + b * uc + sc, l] = 1.0
            place_parts.append(pl_m)
        bf = lambda z: np.asarray(z).astype(jnp.bfloat16)
        out = [bf(np.concatenate(q_parts, 0)), bf(np.concatenate(p_parts, 0))]
        out += [bf(a) for a in a_parts]
        out.append(bf(np.concatenate(place_parts, 0)))

        ky = np.arange(MODES_Y)
        mx = np.arange(MODES_X)
        kx = np.where(mx < MODES_X // 2, mx, mx - MODES_X)
        ty = 2 * np.pi * ((np.arange(cols)[None, :] * ky[:, None]) % cols) / cols
        fct = np.concatenate([np.cos(ty), -np.sin(ty)], 0)
        out.append(np.concatenate(np_split(fct), 0))
        tx = 2 * np.pi * ((np.arange(rows)[:, None] * kx[None, :]) % rows) / rows
        cx, sx = np.cos(tx), np.sin(tx)
        rd = np.zeros((rows, FP, 2, MODES_X, FP))
        for f in range(FP):
            rd[:, f, 0, :, f] = cx
            rd[:, f, 1, :, f] = sx
        rd = rd.reshape(rows * FP, 2 * MODES_X * FP)
        out += list(np_split(rd))
        ir = np.zeros((2, MODES_X, MODES_Y, rows, 2, MODES_Y))
        for y in range(MODES_Y):
            ir[0, :, y, :, 0, y] = cx.T
            ir[0, :, y, :, 1, y] = sx.T
            ir[1, :, y, :, 0, y] = -sx.T
            ir[1, :, y, :, 1, y] = cx.T
        ir = ir.reshape(2 * MODES_X * MODES_Y, rows * 2 * MODES_Y)
        out += list(np_split(ir))
        fold = np.where(ky == 0, 1.0, 2.0)[:, None] / (rows * cols)
        inv = np.concatenate([np.cos(ty) * fold, -np.sin(ty) * fold], 0)
        bd = np.zeros((8, 2 * MODES_Y, 8, cols))
        for g in range(8):
            bd[g, :, g, :] = inv
        bh, bl = np_split(bd.reshape(8 * 2 * MODES_Y, 8 * cols))
        out.append(np.concatenate([bh, bh, bl], 0))
        return out


def twice_gelu(v):
    c = math.sqrt(2.0 / math.pi)
    t = jnp.tanh(v * (c + (0.044715 * c) * (v * v)))
    return v + v * t


def kernel(plan, hid, inn, *refs):
    hbm, out, vm = refs[:24], refs[24], refs[25:49]
    (fields, wbuf, lw, lb, bw, lyb, miw, mib, mow, mob, pw, pb, qm, pm, a1, a2, a3, place, fct, rdh, rdl,
     irh, irl, bd) = vm
    (cur, feat, wsp, vs, pk1, pk2, pk3, u1, u2, u3, r1, r2, r3, lfs, pjs, pbs, wf, win, bcol, wp, lift_h,
     lift_l, csem, ssem, rsem) = refs[49:]
    ch, rows, cols, nx, ny = plan.ch, plan.rows, plan.cols, plan.nx, plan.ny
    ams, pks, us, recvs = (a1, a2, a3), (pk1, pk2, pk3), (u1, u2, u3), (r1, r2, r3)
    ix, iy = lax.axis_index("gx"), lax.axis_index("gy")

    loads = [pltpu.make_async_copy(h, v, csem.at[n]) for n, (h, v) in enumerate(zip(hbm, vm))]
    for n in (0, 12, 13):
        loads[n].start()
    everyone = plan.everyone
    barrier = pltpu.get_barrier_semaphore()
    for a, b in everyone:
        pl.semaphore_signal(barrier, inc=1, device_id=(lax.rem(ix + a, nx), lax.rem(iy + b, ny)),
                            device_id_type=MESH)
    for n in range(2, 12):
        loads[n].start()

    cur[...] = jnp.zeros_like(cur)
    sub = lax.broadcasted_iota(jnp.int32, (rows * FP, cols), 0) % FP
    feat[...] = jnp.where(sub == 4 * ch, 1.0, 0.0).astype(F32)
    for u in us:
        u[...] = jnp.zeros_like(u)
    for n in (0, 12, 13):
        loads[n].wait()
    for c in range(ch):
        cur[pl.ds(c, rows, stride=8), :] = fields[c]

    def pool():
        ch_, cl_ = split(cur[...])
        s = bdot(qm[...], ch_) + bdot(qm[...], cl_)
        sh, sl = split(s)
        start, pstart = 0, 0
        for n, lv in enumerate(plan.lv):
            h, nb, qr, uc = lv["h"], lv["nb"], lv["qrows"], lv["uc"]
            size = h * nb * qr
            lane = lax.broadcasted_iota(jnp.int32, (qr, cols), 1) // uc
            for hy in range(h):
                pmk = pm[pstart:pstart + cols, :]
                pstart += cols
                t = bdot(sh[start:start + size], pmk) + bdot(sl[start:start + size], pmk)
                for hx in range(h):
                    v = t[hx * nb * qr:hx * nb * qr + qr]
                    for b in range(1, nb):
                        o = (hx * nb + b) * qr
                        v = jnp.where(lane == b, t[o:o + qr], v)
                    pks[n][hx * h + hy] = v[0:lv["sr"]]
            start += size

    def send(step):
        for n, slot, a, b in plan.messages:
            lv = plan.lv[n]
            h = lv["h"]
            pltpu.make_async_remote_copy(
                src_ref=pks[n].at[(a % h) * h + b % h, 0:lv["nq"]],
                dst_ref=recvs[n].at[step, slot, 0:lv["nq"]],
                send_sem=ssem.at[step, n], recv_sem=rsem.at[step, n],
                device_id=(lax.rem(ix - a // h + nx, nx), lax.rem(iy - b // h + ny, ny)),
                device_id_type=MESH).start()

    def wait_level(step, sems, n):
        ref = recvs[n].at[step, :, 0:plan.lv[n]["nq"]]
        pltpu.make_async_copy(ref, ref, sems.at[step, n]).wait()

    nf = lw.shape[0]
    hp = functools.partial(jnp.dot, precision=lax.Precision.HIGHEST, preferred_element_type=F32)
    row_of = lambda ref: ref[...].reshape(1, ref.shape[0])
    pool()
    pl.semaphore_wait(barrier, len(everyone))
    send(0)
    for n in (1,) + tuple(range(14, 24)):
        loads[n].start()
    for n in range(2, 12):
        loads[n].wait()
    lfs[...] = jnp.zeros_like(lfs)
    lfs[0:nf, :] = lw[...]
    lfs[nf:nf + 1, :] = row_of(lb)
    lf = lfs[...]
    h, l = split(jnp.concatenate([lf] * MODES_Y, axis=1))
    lift_h[...] = jnp.concatenate([h] * MODES_X, axis=0)
    lift_l[...] = jnp.concatenate([l] * MODES_X, axis=0)
    wb = hp(lf, bw[...])
    wb = wb + jnp.where(lax.broadcasted_iota(jnp.int32, wb.shape, 0) == nf, row_of(lyb), 0.0)
    h, l = split(wb.T)
    wf[...] = jnp.concatenate([h, h, l], axis=1)
    pjs[...] = jnp.zeros_like(pjs)
    pjs[0:ch, 0:hid + inn] = jnp.concatenate([pw[...], hp(pw[...], mow[...])], axis=1)
    pj = pjs[:, 0:hid + inn]
    h, l = split(0.5 * pj)
    wp[...] = jnp.concatenate([h, l], axis=0)
    pbs[...] = jnp.zeros_like(pbs)
    pbs[0:1, 0:inn] = row_of(mib)
    pbs[1:2, 0:ch] = row_of(pb)
    bcol[...] = pbs[...].T
    h, l = split(0.5 * miw[...].T)
    bh, bl = split(bcol[0:inn, 0:1])
    win[...] = jnp.concatenate([h, h, l, bh, bl, jnp.zeros((inn, 14), BF16)], axis=1)
    bcol[0:8, 1:2] = bcol[0:8, 1:2] + jnp.sum(pj[:, 0:hid] * row_of(mob), axis=1, keepdims=True)
    for step in range(STEPS):
        if step > 0:
            send(step)
        if step == 0:
            loads[1].wait()
            for m in range(MODES_X):
                w = jnp.concatenate(
                    [wbuf[part, m].reshape(MODES_Y * hid, hid) for part in range(2)], axis=1)
                wh, wl = split(w)
                wsp[m, :, 0:2 * hid] = wh
                wsp[m, :, 2 * hid:4 * hid] = wl
            for n in range(14, 24):
                loads[n].wait()
        for r in range(rows):
            feat[r * FP:r * FP + 8, :] = jnp.where(
                lax.broadcasted_iota(jnp.int32, (8, cols), 0) < ch, cur[r * 8:(r + 1) * 8, :],
                feat[r * FP:r * FP + 8, :])
        starts = [sum(len(q["dys"]) for q in plan.lv[:n]) * cols for n in range(len(plan.lv))]
        for n in (0, 1, 2):
            lv = plan.lv[n]
            start = starts[n]
            p, h, sr, ur, uc, nq = (lv[x] for x in ("p", "h", "sr", "ur", "uc", "nq"))
            u = us[n]
            wait_level(step, rsem, n)
            for x, a in enumerate(lv["dxs"]):
                for y, b in enumerate(lv["dys"]):
                    own = (a // h, b // h) == (0, 0)
                    block = pks[n][a * h + b, 0:nq] if own else recvs[n][step, lv["index"][a, b], 0:nq]
                    u[x * sr:x * sr + nq, y * cols:(y + 1) * cols] = block
            uh, ul = split(u[...])
            eh, el = bdot(ams[n][...], uh), bdot(ams[n][...], ul)
            width = len(lv["dys"]) * cols
            row = lax.broadcasted_iota(jnp.int32, (ch * rows, width), 0)
            lane = lax.broadcasted_iota(jnp.int32, (ch * rows, width), 1)
            wpos = row % rows + (lv["r0"] + p * p * ur)
            rho = (row // rows) * ur + wpos % ur
            keep = (lane % cols) // uc == rho // nq
            e = jnp.concatenate(
                [jnp.where(keep, eh, 0.0).astype(BF16), jnp.where(keep, el, 0.0).astype(BF16)], axis=0)
            ctx = bdot(e, place[start:start + width, :])
            ctx = ctx[:ch * rows] + ctx[ch * rows:]
            for c in range(ch):
                feat[pl.ds(ch * (n + 1) + c, rows, stride=FP), :] = ctx[c * rows:(c + 1) * rows]
        fh, fl = split(feat[...])
        y2 = ntdot(fct[...], fh)
        yy = y2[0:16] + y2[16:32] + ntdot(fct[0:16, :], fl)
        yh, yl = split(yy)
        z2 = bdot(jnp.concatenate([yh, yl], axis=0), rdh[...])
        z = z2[0:16] + z2[16:32] + bdot(yh, rdl[...])
        half = MODES_X * FP
        zc, zs = z[:, :half], z[:, half:]
        hf = jnp.concatenate([zc[0:8] + zs[8:16], zc[8:16] - zs[0:8]], axis=0)
        t = jnp.concatenate([hf] * MODES_X, axis=0)
        rr = lax.broadcasted_iota(jnp.int32, t.shape, 0) // 16
        ll = lax.broadcasted_iota(jnp.int32, t.shape, 1) // FP
        th, tl = split(jnp.where(rr == ll, t, 0.0))
        h2 = bdot(jnp.concatenate([th, tl], axis=0), lift_h[...])
        nm = MODES_X * 16
        hl = h2[:nm] + h2[nm:] + bdot(th, lift_l[...])
        rr = lax.broadcasted_iota(jnp.int32, hl.shape, 0) % 8
        ll = lax.broadcasted_iota(jnp.int32, hl.shape, 1) // hid
        hh, hlo = split(jnp.where(rr == ll, hl, 0.0))
        gre, gim = [], []
        first = lax.broadcasted_iota(jnp.int32, (8, 2 * hid), 1) < hid
        for m in range(MODES_X):
            lhs = jnp.concatenate([hh[m * 16:(m + 1) * 16], hlo[m * 16:(m + 1) * 16]], axis=0)
            v = bdot(lhs, wsp[m])
            v = v[0:16, 0:2 * hid] + v[16:32, 0:2 * hid] + v[0:16, 2 * hid:4 * hid]
            turned = pltpu.roll(v[8:16], hid, 1)
            both = v[0:8] + jnp.where(first, -turned, turned)
            gre.append(both[:, 0:hid])
            gim.append(pltpu.roll(both, hid, 1)[:, 0:hid])
        g = jnp.concatenate(gre + gim, axis=0)
        gh, gl = split(g.T)
        b2 = bdot(jnp.concatenate([gh, gl], axis=0), irh[...])
        ball = b2[:hid] + b2[hid:] + bdot(gh, irl[...])
        bh, bl = split(ball)
        stack = lambda q: jnp.concatenate(
            [q[:, k * 128:(k + 1) * 128] for k in range(rows // 8)], axis=0)
        bh, bl = stack(bh), stack(bl)
        vs[...] = bdot(jnp.concatenate([bh, bl, bh], axis=1), bd[...])
        ones = jnp.where(lax.broadcasted_iota(jnp.int32, (16, rows * cols), 0) < 2, 1.0, 0.0).astype(BF16)
        for blk in range(rows // rows):
            r0 = blk * rows
            cat = lambda q: jnp.concatenate(
                [q[(r0 + k) * FP:(r0 + k + 1) * FP] for k in range(rows)], axis=1)
            fhc, flc = cat(fh), cat(fl)
            v = jnp.concatenate([vs[(r0 // 8 + j) * hid:(r0 // 8 + j + 1) * hid, :] for j in range(rows // 8)], axis=1)
            v = v + bdot(wf[...], jnp.concatenate([fhc, flc, fhc], axis=0))
            mh, ml = split(twice_gelu(v))
            ih, il = split(twice_gelu(bdot(win[...], jnp.concatenate([mh, ml, mh, ones], axis=0))))
            o2 = bdot(wp[...], jnp.concatenate([mh, ih], axis=0))
            o1 = bdot(wp[...], jnp.concatenate([ml, il], axis=0))
            ov = o2[0:8] + o2[8:16] + o1[0:8] + bcol[0:8, 1:2]
            for k in range(rows):
                cur[(r0 + k) * 8:(r0 + k + 1) * 8, :] += ov[:, k * cols:(k + 1) * cols]
        for n in range(len(plan.lv)):
            wait_level(step, ssem, n)
        if step < STEPS - 1:
            pool()
    for c in range(ch):
        out[c] = cur[pl.ds(c, rows, stride=8), :]


def shards(plan, fields, lift_weight, lift_bias, spectral_weight, bypass_weight, layer_bias, mlp_in_weight,
           mlp_in_bias, mlp_out_weight, mlp_out_bias, project_weight, project_bias):
    ch, rows, cols = fields.shape
    hid = lift_weight.shape[1]
    inn = mlp_in_weight.shape[1]
    consts = [jnp.asarray(c) for c in plan.constants()]
    args = [fields, spectral_weight, lift_weight, lift_bias, bypass_weight, layer_bias, mlp_in_weight,
            mlp_in_bias, mlp_out_weight.T, mlp_out_bias, project_weight.T, project_bias] + consts
    assert len(args) == 24
    scratch = [pltpu.VMEM(a.shape, a.dtype) for a in args]
    scratch += [
        pltpu.VMEM((rows * 8, cols), F32),
        pltpu.VMEM((rows * FP, cols), F32),
        pltpu.VMEM((MODES_X, MODES_Y * hid, 4 * hid), BF16),
        pltpu.VMEM((rows // 8 * hid, 8 * cols), F32),
    ]
    scratch += [pltpu.VMEM((lv["h"] ** 2, lv["sr"], cols), F32) for lv in plan.lv]
    scratch += [pltpu.VMEM((lv["kpad"], len(lv["dys"]) * cols), F32) for lv in plan.lv]
    scratch += [pltpu.VMEM((STEPS, len(lv["slots"]), lv["sr"], cols), F32) for lv in plan.lv]
    wide = round_up(max(inn, cols), 128)
    scratch += [
        pltpu.VMEM((FP, hid), F32),
        pltpu.VMEM((8, round_up(hid + inn, 128)), F32),
        pltpu.VMEM((8, wide), F32),
        pltpu.VMEM((hid, 3 * FP), BF16),
        pltpu.VMEM((inn, 3 * hid + 16), BF16),
        pltpu.VMEM((wide, 8), F32),
        pltpu.VMEM((16, hid + inn), BF16),
        pltpu.VMEM((MODES_X * FP, MODES_Y * hid), BF16),
        pltpu.VMEM((MODES_X * FP, MODES_Y * hid), BF16),
    ]
    scratch += [pltpu.SemaphoreType.DMA((len(args),)), pltpu.SemaphoreType.DMA((STEPS, len(plan.lv))),
                pltpu.SemaphoreType.DMA((STEPS, len(plan.lv)))]
    return pl.pallas_call(
        functools.partial(kernel, plan, hid, inn),
        out_shape=pltpu.VMEM(fields.shape, F32),
        in_specs=[pl.BlockSpec(memory_space=pl.ANY)] * len(args),
        out_specs=pl.BlockSpec(memory_space=pltpu.VMEM),
        scratch_shapes=scratch,
        compiler_params=pltpu.CompilerParams(collective_id=0, has_side_effects=True,
                                             vmem_limit_bytes=60 * 1024 * 1024),
    )(*args)


def solution(mesh):
    nx, ny = mesh.shape["gx"], mesh.shape["gy"]

    def body(fields, *rest):
        plan = Plan(*fields.shape, nx, ny)
        return shards(plan, fields, *rest)

    placed = (P(None, "gx", "gy"),) + (P(),) * 11
    return jax.shard_map(body, mesh=mesh, in_specs=placed, out_specs=P(None, "gx", "gy"), check_vma=False)
```

```python
import functools
import math

import jax
import jax.numpy as jnp
import numpy as np
from jax import lax
from jax.experimental import pallas as pl
from jax.experimental.pallas import tpu as pltpu
from jax.sharding import PartitionSpec as P

MODES_X = 8
MODES_Y = 8
STEPS = 2
LEVELS = (1, 2, 3)
F32 = jnp.float32
BF16 = jnp.bfloat16
FP = 16
MESH = pl.DeviceIdType.MESH


def np_split(a):
    a = np.asarray(a, np.float32)
    hi = a.astype(jnp.bfloat16)
    lo = (a - hi.astype(np.float32)).astype(jnp.bfloat16)
    return hi, lo


def split(x):
    hi = x.astype(BF16)
    lo = (x - hi.astype(F32)).astype(BF16)
    return hi, lo


def bdot(a, b):
    return jnp.dot(a, b, preferred_element_type=F32)


def round_up(n, m):
    return -(-n // m) * m


class Plan:
    def __init__(self, ch, rows, cols, nx, ny):
        self.ch, self.rows, self.cols, self.nx, self.ny = ch, rows, cols, nx, ny
        self.lv = []
        for k in LEVELS:
            p = 2**k
            h = 2 if k == 1 else 1
            nr, nc = rows // p, cols // p
            ur, uc = nr // h, nc // h
            nb = cols // uc
            nq = -(-ch * ur // nb)
            slot_rows = nq if nq in (1, 2, 4) else round_up(nq, 8)
            r0, c0 = -(p - 1) * nr // 2, -(p - 1) * nc // 2
            dxs = sorted({d % (h * nx) for d in range(r0 // ur, (r0 + rows - 1) // ur + 1)})
            dys = sorted({d % (h * ny) for d in range(c0 // uc, (c0 + cols - 1) // uc + 1)})
            slots = [(a, b) for a in dxs for b in dys if (a // h, b // h) != (0, 0)]
            kpad = round_up(len(dxs) * slot_rows, 16)
            self.lv.append(
                dict(p=p, h=h, ur=ur, uc=uc, nb=nb, nq=nq, sr=slot_rows, r0=r0, c0=c0, dxs=dxs, dys=dys,
                     slots=slots, index={q: n for n, q in enumerate(slots)}, kpad=kpad,
                     qrows=round_up(nq, 8))
            )
        def far(m):
            h = self.lv[m[0]]["h"]
            da, db = (m[2] // h) % nx, (m[3] // h) % ny
            return min(da, nx - da) + min(db, ny - db)

        self.messages = sorted(
            ((n, slot, a, b) for n, lv in enumerate(self.lv) for slot, (a, b) in enumerate(lv["slots"])),
            key=lambda m: m[0])
        offs = {(a // lv["h"], b // lv["h"]) for lv in self.lv for a, b in lv["slots"]}
        self.everyone = sorted(offs | {((-a) % nx, (-b) % ny) for a, b in offs})

    def constants(self):
        ch, rows, cols = self.ch, self.rows, self.cols
        q_parts, p_parts, a_parts, place_parts = [], [], [], []
        for lv in self.lv:
            p, h, ur, uc, nb, nq, qr = (lv[x] for x in ("p", "h", "ur", "uc", "nb", "nq", "qrows"))
            q = np.zeros((h, nb, qr, rows * 8), np.float32)
            for hx in range(h):
                for b in range(nb):
                    for t in range(nq):
                        rho = b * nq + t
                        if rho < ch * ur:
                            c, rr = divmod(rho, ur)
                            for u in range(p):
                                q[hx, b, t, ((hx * ur + rr) * p + u) * 8 + c] = 1.0 / p
            q_parts.append(q.reshape(h * nb * qr, rows * 8))
            for hy in range(h):
                pm = np.zeros((cols, cols), np.float32)
                for j in range(uc):
                    for b in range(nb):
                        pm[(hy * uc + j) * p:(hy * uc + j + 1) * p, b * uc + j] = 1.0 / p
                p_parts.append(pm)
            a = np.zeros((ch * rows, lv["kpad"]), np.float32)
            for c in range(ch):
                for w in range(rows):
                    d, rr = divmod(w + lv["r0"], ur)
                    t = (c * ur + rr) % nq
                    a[c * rows + w, lv["dxs"].index(d % (h * self.nx)) * lv["sr"] + t] = 1.0
            a_parts.append(a)
            pl_m = np.zeros((len(lv["dys"]) * cols, cols), np.float32)
            for l in range(cols):
                d, sc = divmod(l + lv["c0"], uc)
                y = lv["dys"].index(d % (h * self.ny))
                for b in range(nb):
                    pl_m[y * cols + b * uc + sc, l] = 1.0
            place_parts.append(pl_m)
        bf = lambda z: np.asarray(z).astype(jnp.bfloat16)
        out = [bf(np.concatenate(q_parts, 0)), bf(np.concatenate(p_parts, 0))]
        out += [bf(a) for a in a_parts]
        out.append(bf(np.concatenate(place_parts, 0)))

        ky = np.arange(MODES_Y)
        mx = np.arange(MODES_X)
        kx = np.where(mx < MODES_X // 2, mx, mx - MODES_X)
        ty = 2 * np.pi * ((np.arange(cols)[None, :] * ky[:, None]) % cols) / cols
        wide = np.concatenate([np.tile(np.cos(ty).T, (1, 2 * MODES_X)), np.tile(np.sin(ty).T, (1, 2 * MODES_X))], 1)
        dh, dl = np_split(wide)
        out.append(np.concatenate([dh, dh, dl], 0))
        tx = 2 * np.pi * ((np.arange(rows)[:, None] * kx[None, :]) % rows) / rows
        cx, sx = np.cos(tx), np.sin(tx)
        cr, sr = np.repeat(cx, MODES_Y, axis=1), np.repeat(sx, MODES_Y, axis=1)
        out.append(np.concatenate([np.concatenate([cr, -sr], 1), np.concatenate([-sr, -cr], 1)], 0).astype(np.float32))
        ir = np.zeros((2, MODES_X, MODES_Y, rows, 2, MODES_Y))
        for y in range(MODES_Y):
            ir[0, :, y, :, 0, y] = cx.T
            ir[0, :, y, :, 1, y] = sx.T
            ir[1, :, y, :, 0, y] = -sx.T
            ir[1, :, y, :, 1, y] = cx.T
        ir = ir.reshape(2 * MODES_X * MODES_Y, rows * 2 * MODES_Y)
        ih, il = np_split(ir)
        out.append(np.concatenate([ih, ih, il], 0))
        fold = SCALE * np.where(ky == 0, 1.0, 2.0)[:, None] / (rows * cols)
        inv = np.concatenate([np.cos(ty) * fold, -np.sin(ty) * fold], 0)
        bd = np.zeros((8, 2 * MODES_Y, 8, cols))
        for g in range(8):
            bd[g, :, g, :] = inv
        bh, bl = np_split(bd.reshape(8 * 2 * MODES_Y, 8 * cols))
        out.append(np.concatenate([bh, bh, bl], 0))
        return out


LINEAR = math.sqrt(2.0 / math.pi)
SCALE = (0.044715 * LINEAR) ** (1.0 / 3.0)
SHIFT = LINEAR / SCALE


def scaled_gelu(w):
    return w + w * jnp.tanh(w * (w * w + SHIFT))


def kernel(plan, hid, inn, *refs):
    hbm, out, vm = refs[:22], refs[22], refs[23:45]
    (fields, wbuf, lw, lb, bw, lyb, miw, mib, mow, mob, pw, pb, qm, pm, a1, a2, a3, place, dft, tw, ir, bd) = vm
    (cur, feat, lwm, lwt, vs, pk1, pk2, pk3, u1, u2, u3, r1, r2, r3, lfs, pjs, pbs, wf, win, bcol, wp, lift_b,
     csem, ssem, rsem) = refs[45:]
    lanes = MODES_X * MODES_Y
    ch, rows, cols, nx, ny = plan.ch, plan.rows, plan.cols, plan.nx, plan.ny
    ams, pks, us, recvs = (a1, a2, a3), (pk1, pk2, pk3), (u1, u2, u3), (r1, r2, r3)
    ix, iy = lax.axis_index("gx"), lax.axis_index("gy")

    loads = [pltpu.make_async_copy(h, v, csem.at[n]) for n, (h, v) in enumerate(zip(hbm, vm))]
    for n in (0, 12, 13):
        loads[n].start()
    everyone = plan.everyone
    barrier = pltpu.get_barrier_semaphore()
    for a, b in everyone:
        pl.semaphore_signal(barrier, inc=1, device_id=(lax.rem(ix + a, nx), lax.rem(iy + b, ny)),
                            device_id_type=MESH)
    for n in tuple(range(2, 12)) + (1,) + tuple(range(14, 22)):
        loads[n].start()

    cur[...] = jnp.zeros_like(cur)
    sub = lax.broadcasted_iota(jnp.int32, (rows * FP, cols), 0) % FP
    feat[...] = jnp.where(sub == 4 * ch, 1.0, 0.0).astype(F32)
    for u in us:
        u[...] = jnp.zeros_like(u)
    for n in (0, 12, 13):
        loads[n].wait()
    for c in range(ch):
        cur[pl.ds(c, rows, stride=8), :] = fields[c]

    def pool():
        ch_, cl_ = split(cur[...])
        s = bdot(qm[...], ch_) + bdot(qm[...], cl_)
        sh, sl = split(s)
        start, pstart = 0, 0
        for n, lv in enumerate(plan.lv):
            h, nb, qr, uc = lv["h"], lv["nb"], lv["qrows"], lv["uc"]
            size = h * nb * qr
            lane = lax.broadcasted_iota(jnp.int32, (qr, cols), 1) // uc
            for hy in range(h):
                pmk = pm[pstart:pstart + cols, :]
                pstart += cols
                t = bdot(sh[start:start + size], pmk) + bdot(sl[start:start + size], pmk)
                for hx in range(h):
                    v = t[hx * nb * qr:hx * nb * qr + qr]
                    for b in range(1, nb):
                        o = (hx * nb + b) * qr
                        v = jnp.where(lane == b, t[o:o + qr], v)
                    pks[n][hx * h + hy] = v[0:lv["sr"]]
            start += size

    def send(step):
        for n, slot, a, b in plan.messages:
            lv = plan.lv[n]
            h = lv["h"]
            pltpu.make_async_remote_copy(
                src_ref=pks[n].at[(a % h) * h + b % h, 0:lv["nq"]],
                dst_ref=recvs[n].at[step, slot, 0:lv["nq"]],
                send_sem=ssem.at[step, n], recv_sem=rsem.at[step, n],
                device_id=(lax.rem(ix - a // h + nx, nx), lax.rem(iy - b // h + ny, ny)),
                device_id_type=MESH).start()

    def wait_level(step, sems, n):
        ref = recvs[n].at[step, :, 0:plan.lv[n]["nq"]]
        pltpu.make_async_copy(ref, ref, sems.at[step, n]).wait()

    nf = lw.shape[0]
    hp = functools.partial(jnp.dot, precision=lax.Precision.HIGHEST, preferred_element_type=F32)
    row_of = lambda ref: ref[...].reshape(1, ref.shape[0])
    pool()
    pl.semaphore_wait(barrier, len(everyone))
    send(0)
    for n in range(2, 12):
        loads[n].wait()
    lfs[...] = jnp.zeros_like(lfs)
    lfs[0:nf, :] = lw[...]
    lfs[nf:nf + 1, :] = row_of(lb)
    lf = lfs[...]
    fr = lift_b.shape[0] // 2
    t = jnp.concatenate([jnp.broadcast_to(lf[f:f + 1], (MODES_Y, hid)) for f in range(fr // MODES_Y)], axis=0)
    t = jnp.concatenate([t] * MODES_Y, axis=1)
    rr = lax.broadcasted_iota(jnp.int32, t.shape, 0) % MODES_Y
    ll = lax.broadcasted_iota(jnp.int32, t.shape, 1) // hid
    h, l = split(jnp.where(rr == ll, t, 0.0))
    lift_b[0:fr, :] = h
    lift_b[fr:2 * fr, :] = l
    wb = hp(lf, bw[...])
    wb = wb + jnp.where(lax.broadcasted_iota(jnp.int32, wb.shape, 0) == nf, row_of(lyb), 0.0)
    h, l = split(SCALE * wb.T)
    wf[...] = jnp.concatenate([h, h, l], axis=1)
    pjs[...] = jnp.zeros_like(pjs)
    pjs[0:ch, 0:hid + inn] = jnp.concatenate([pw[...], hp(pw[...], mow[...])], axis=1)
    pj = pjs[:, 0:hid + inn]
    h, l = split((0.5 / SCALE) * pj)
    wp[...] = jnp.concatenate([h, l], axis=0)
    pbs[...] = jnp.zeros_like(pbs)
    pbs[0:1, 0:inn] = row_of(mib)
    pbs[1:2, 0:ch] = row_of(pb)
    bcol[...] = pbs[...].T
    h, l = split(0.5 * miw[...].T)
    bh, bl = split(SCALE * bcol[0:inn, 0:1])
    win[...] = jnp.concatenate([h, h, l, bh, bl, jnp.zeros((inn, 14), BF16)], axis=1)
    bcol[0:8, 1:2] = bcol[0:8, 1:2] + jnp.sum(pj[:, 0:hid] * row_of(mob), axis=1, keepdims=True)
    for step in range(STEPS):
        if step > 0:
            send(step)
        if step == 0:
            loads[1].wait()
            for m in range(MODES_X):
                w = jnp.concatenate(
                    [wbuf[part, m].reshape(MODES_Y * hid, hid) for part in range(2)], axis=1)
                wh, wl = split(w)
                q = bdot(lift_b[...], jnp.concatenate([wh, wl], axis=1))
                lwm[m] = q[0:fr, 0:2 * hid] + q[fr:, 0:2 * hid] + q[0:fr, 2 * hid:4 * hid]
            for f in range(nf + 1):
                t = lwm[:, f * MODES_Y:(f + 1) * MODES_Y, :].reshape(lanes, 2 * hid).T
                lwt[f] = jnp.concatenate([t[0:hid], t[hid:2 * hid]], axis=1)
            for n in range(14, 22):
                loads[n].wait()
        for r in range(rows):
            feat[r * FP:r * FP + 8, :] = jnp.where(
                lax.broadcasted_iota(jnp.int32, (8, cols), 0) < ch, cur[r * 8:(r + 1) * 8, :],
                feat[r * FP:r * FP + 8, :])
        starts = [sum(len(q["dys"]) for q in plan.lv[:n]) * cols for n in range(len(plan.lv))]
        for n in (0, 1, 2):
            lv = plan.lv[n]
            start = starts[n]
            p, h, sr, ur, uc, nq = (lv[x] for x in ("p", "h", "sr", "ur", "uc", "nq"))
            u = us[n]
            wait_level(step, rsem, n)
            for x, a in enumerate(lv["dxs"]):
                for y, b in enumerate(lv["dys"]):
                    own = (a // h, b // h) == (0, 0)
                    block = pks[n][a * h + b, 0:nq] if own else recvs[n][step, lv["index"][a, b], 0:nq]
                    u[x * sr:x * sr + nq, y * cols:(y + 1) * cols] = block
            uh, ul = split(u[...])
            eh, el = bdot(ams[n][...], uh), bdot(ams[n][...], ul)
            width = len(lv["dys"]) * cols
            row = lax.broadcasted_iota(jnp.int32, (ch * rows, width), 0)
            lane = lax.broadcasted_iota(jnp.int32, (ch * rows, width), 1)
            wpos = row % rows + (lv["r0"] + p * p * ur)
            rho = (row // rows) * ur + wpos % ur
            keep = (lane % cols) // uc == rho // nq
            e = jnp.concatenate(
                [jnp.where(keep, eh, 0.0).astype(BF16), jnp.where(keep, el, 0.0).astype(BF16)], axis=0)
            ctx = bdot(e, place[start:start + width, :])
            ctx = ctx[:ch * rows] + ctx[ch * rows:]
            for c in range(ch):
                feat[pl.ds(ch * (n + 1) + c, rows, stride=FP), :] = ctx[c * rows:(c + 1) * rows]
        fh, fl = split(feat[...])
        z = bdot(jnp.concatenate([fh, fl, fh], axis=1), dft[...])
        parts = []
        for r in range(rows):
            zr = z[r * FP:(r + 1) * FP]
            parts.append(zr[:, 0:2 * lanes] * tw[r:r + 1, :] + zr[:, 2 * lanes:4 * lanes] * tw[rows + r:rows + r + 1, :])
        while len(parts) > 1:
            parts = [a + b for a, b in zip(parts[0::2], parts[1::2])] + ([parts[-1]] if len(parts) % 2 else [])
        hf = parts[0]
        turned = pltpu.roll(hf, lanes, 1)
        first = lax.broadcasted_iota(jnp.int32, hf.shape, 1) < lanes
        f1, f2 = jnp.where(first, hf, turned), jnp.where(first, turned, -hf)
        ga = sum(f1[f:f + 1] * lwt[f] for f in range(nf + 1))
        gb = sum(f2[f:f + 1] * lwt[f] for f in range(nf + 1))
        gh, gl = split(ga + pltpu.roll(gb, lanes, 1))
        ball = bdot(jnp.concatenate([gh, gl, gh], axis=1), ir[...])
        bh, bl = split(ball)
        stack = lambda q: jnp.concatenate(
            [q[:, k * 128:(k + 1) * 128] for k in range(rows // 8)], axis=0)
        bh, bl = stack(bh), stack(bl)
        vs[...] = bdot(jnp.concatenate([bh, bl, bh], axis=1), bd[...])
        ones = jnp.where(lax.broadcasted_iota(jnp.int32, (16, rows * cols), 0) < 2, 1.0, 0.0).astype(BF16)
        for blk in range(rows // rows):
            r0 = blk * rows
            cat = lambda q: jnp.concatenate(
                [q[(r0 + k) * FP:(r0 + k + 1) * FP] for k in range(rows)], axis=1)
            fhc, flc = cat(fh), cat(fl)
            v = jnp.concatenate([vs[(r0 // 8 + j) * hid:(r0 // 8 + j + 1) * hid, :] for j in range(rows // 8)], axis=1)
            v = v + bdot(wf[...], jnp.concatenate([fhc, flc, fhc], axis=0))
            mh, ml = split(scaled_gelu(v))
            ih, il = split(scaled_gelu(bdot(win[...], jnp.concatenate([mh, ml, mh, ones], axis=0))))
            o2 = bdot(wp[...], jnp.concatenate([mh, ih], axis=0))
            o1 = bdot(wp[...], jnp.concatenate([ml, il], axis=0))
            ov = o2[0:8] + o2[8:16] + o1[0:8] + bcol[0:8, 1:2]
            for k in range(rows):
                cur[(r0 + k) * 8:(r0 + k + 1) * 8, :] += ov[:, k * cols:(k + 1) * cols]
        for n in range(len(plan.lv)):
            wait_level(step, ssem, n)
        if step < STEPS - 1:
            pool()
    for c in range(ch):
        out[c] = cur[pl.ds(c, rows, stride=8), :]


def shards(plan, fields, lift_weight, lift_bias, spectral_weight, bypass_weight, layer_bias, mlp_in_weight,
           mlp_in_bias, mlp_out_weight, mlp_out_bias, project_weight, project_bias):
    ch, rows, cols = fields.shape
    hid = lift_weight.shape[1]
    inn = mlp_in_weight.shape[1]
    consts = [jnp.asarray(c) for c in plan.constants()]
    args = [fields, spectral_weight, lift_weight, lift_bias, bypass_weight, layer_bias, mlp_in_weight,
            mlp_in_bias, mlp_out_weight.T, mlp_out_bias, project_weight.T, project_bias] + consts
    assert len(args) == 22
    scratch = [pltpu.VMEM(a.shape, a.dtype) for a in args]
    fr = round_up(4 * ch + 1, 2) * MODES_Y
    scratch += [
        pltpu.VMEM((rows * 8, cols), F32),
        pltpu.VMEM((rows * FP, cols), F32),
        pltpu.VMEM((MODES_X, fr, 2 * hid), F32),
        pltpu.VMEM((4 * ch + 1, hid, 2 * MODES_X * MODES_Y), F32),
        pltpu.VMEM((rows // 8 * hid, 8 * cols), F32),
    ]
    scratch += [pltpu.VMEM((lv["h"] ** 2, lv["sr"], cols), F32) for lv in plan.lv]
    scratch += [pltpu.VMEM((lv["kpad"], len(lv["dys"]) * cols), F32) for lv in plan.lv]
    scratch += [pltpu.VMEM((STEPS, len(lv["slots"]), lv["sr"], cols), F32) for lv in plan.lv]
    wide = round_up(max(inn, cols), 128)
    scratch += [
        pltpu.VMEM((FP, hid), F32),
        pltpu.VMEM((8, round_up(hid + inn, 128)), F32),
        pltpu.VMEM((8, wide), F32),
        pltpu.VMEM((hid, 3 * FP), BF16),
        pltpu.VMEM((inn, 3 * hid + 16), BF16),
        pltpu.VMEM((wide, 8), F32),
        pltpu.VMEM((16, hid + inn), BF16),
        pltpu.VMEM((2 * fr, MODES_Y * hid), BF16),
    ]
    scratch += [pltpu.SemaphoreType.DMA((len(args),)), pltpu.SemaphoreType.DMA((STEPS, len(plan.lv))),
                pltpu.SemaphoreType.DMA((STEPS, len(plan.lv)))]
    return pl.pallas_call(
        functools.partial(kernel, plan, hid, inn),
        out_shape=pltpu.VMEM(fields.shape, F32),
        in_specs=[pl.BlockSpec(memory_space=pl.ANY)] * len(args),
        out_specs=pl.BlockSpec(memory_space=pltpu.VMEM),
        scratch_shapes=scratch,
        compiler_params=pltpu.CompilerParams(collective_id=0, has_side_effects=True,
                                             vmem_limit_bytes=60 * 1024 * 1024),
    )(*args)


def solution(mesh):
    nx, ny = mesh.shape["gx"], mesh.shape["gy"]

    def body(fields, *rest):
        plan = Plan(*fields.shape, nx, ny)
        return shards(plan, fields, *rest)

    placed = (P(None, "gx", "gy"),) + (P(),) * 11
    return jax.shard_map(body, mesh=mesh, in_specs=placed, out_specs=P(None, "gx", "gy"), check_vma=False)
```

```python
import functools
import math

import jax
import jax.numpy as jnp
import numpy as np
from jax import lax
from jax.experimental import pallas as pl
from jax.experimental.pallas import tpu as pltpu
from jax.sharding import PartitionSpec as P

MODES_X = 8
MODES_Y = 8
STEPS = 2
LEVELS = (1, 2, 3)
F32 = jnp.float32
BF16 = jnp.bfloat16
FP = 16
MESH = pl.DeviceIdType.MESH


def np_split(a):
    a = np.asarray(a, np.float32)
    hi = a.astype(jnp.bfloat16)
    lo = (a - hi.astype(np.float32)).astype(jnp.bfloat16)
    return hi, lo


def split(x):
    hi = x.astype(BF16)
    lo = (x - hi.astype(F32)).astype(BF16)
    return hi, lo


def bdot(a, b):
    return jnp.dot(a, b, preferred_element_type=F32)


def round_up(n, m):
    return -(-n // m) * m


class Plan:
    def __init__(self, ch, rows, cols, nx, ny):
        self.ch, self.rows, self.cols, self.nx, self.ny = ch, rows, cols, nx, ny
        self.lv = []
        for k in LEVELS:
            p = 2**k
            h = 2 if k == 1 else 1
            nr, nc = rows // p, cols // p
            ur, uc = nr // h, nc // h
            nb = cols // uc
            nq = -(-ch * ur // nb)
            slot_rows = nq if nq in (1, 2, 4) else round_up(nq, 8)
            r0, c0 = -(p - 1) * nr // 2, -(p - 1) * nc // 2
            dxs = sorted({d % (h * nx) for d in range(r0 // ur, (r0 + rows - 1) // ur + 1)})
            dys = sorted({d % (h * ny) for d in range(c0 // uc, (c0 + cols - 1) // uc + 1)})
            slots = [(a, b) for a in dxs for b in dys if (a // h, b // h) != (0, 0)]
            kpad = round_up(len(dxs) * slot_rows, 16)
            self.lv.append(
                dict(p=p, h=h, ur=ur, uc=uc, nb=nb, nq=nq, sr=slot_rows, r0=r0, c0=c0, dxs=dxs, dys=dys,
                     slots=slots, index={q: n for n, q in enumerate(slots)}, kpad=kpad,
                     qrows=round_up(nq, 8))
            )
        def hops(a, b):
            mx = max(nx // 2, 1)
            gx = max(abs(i // mx - (i + a) % nx // mx) + abs(i % mx - (i + a) % nx % mx) for i in range(nx))
            gy = max(abs(j // 2 - (j + b) % ny // 2) for j in range(ny))
            return gx + gy

        def far(m):
            h = self.lv[m[0]]["h"]
            return hops((-(m[2] // h)) % nx, (-(m[3] // h)) % ny)

        self.messages = sorted(
            ((n, slot, a, b) for n, lv in enumerate(self.lv) for slot, (a, b) in enumerate(lv["slots"])),
            key=lambda m: (-far(m), m[0]))
        offs = {(a // lv["h"], b // lv["h"]) for lv in self.lv for a, b in lv["slots"]}
        self.everyone = sorted(offs | {((-a) % nx, (-b) % ny) for a, b in offs}, key=lambda q: (-hops(*q), q))

    def constants(self):
        ch, rows, cols = self.ch, self.rows, self.cols
        q_parts, p_parts, a_parts, place_parts = [], [], [], []
        for lv in self.lv:
            p, h, ur, uc, nb, nq, qr = (lv[x] for x in ("p", "h", "ur", "uc", "nb", "nq", "qrows"))
            q = np.zeros((h, nb, qr, rows * 8), np.float32)
            for hx in range(h):
                for b in range(nb):
                    for t in range(nq):
                        rho = b * nq + t
                        if rho < ch * ur:
                            c, rr = divmod(rho, ur)
                            for u in range(p):
                                q[hx, b, t, ((hx * ur + rr) * p + u) * 8 + c] = 1.0 / p
            q_parts.append(q.reshape(h * nb * qr, rows * 8))
            for hy in range(h):
                pm = np.zeros((cols, cols), np.float32)
                for j in range(uc):
                    for b in range(nb):
                        pm[(hy * uc + j) * p:(hy * uc + j + 1) * p, b * uc + j] = 1.0 / p
                p_parts.append(pm)
            a = np.zeros((ch * rows, lv["kpad"]), np.float32)
            for c in range(ch):
                for w in range(rows):
                    d, rr = divmod(w + lv["r0"], ur)
                    t = (c * ur + rr) % nq
                    a[c * rows + w, lv["dxs"].index(d % (h * self.nx)) * lv["sr"] + t] = 1.0
            a_parts.append(a)
            pl_m = np.zeros((len(lv["dys"]) * cols, cols), np.float32)
            for l in range(cols):
                d, sc = divmod(l + lv["c0"], uc)
                y = lv["dys"].index(d % (h * self.ny))
                for b in range(nb):
                    pl_m[y * cols + b * uc + sc, l] = 1.0
            place_parts.append(pl_m)
        bf = lambda z: np.asarray(z).astype(jnp.bfloat16)
        out = [bf(np.concatenate(q_parts, 0)), bf(np.concatenate(p_parts, 0))]
        out += [bf(a) for a in a_parts]
        out.append(bf(np.concatenate(place_parts, 0)))

        ky = np.arange(MODES_Y)
        mx = np.arange(MODES_X)
        kx = np.where(mx < MODES_X // 2, mx, mx - MODES_X)
        ty = 2 * np.pi * ((np.arange(cols)[None, :] * ky[:, None]) % cols) / cols
        wide = np.concatenate([np.tile(np.cos(ty).T, (1, 2 * MODES_X)), np.tile(np.sin(ty).T, (1, 2 * MODES_X))], 1)
        dh, dl = np_split(wide)
        out.append(np.concatenate([dh, dh, dl], 0))
        tx = 2 * np.pi * ((np.arange(rows)[:, None] * kx[None, :]) % rows) / rows
        cx, sx = np.cos(tx), np.sin(tx)
        cr, sr = np.repeat(cx, MODES_Y, axis=1), np.repeat(sx, MODES_Y, axis=1)
        out.append(np.concatenate([np.concatenate([cr, -sr], 1), np.concatenate([-sr, -cr], 1)], 0).astype(np.float32))
        ir = np.zeros((2, MODES_X, MODES_Y, rows, 2, MODES_Y))
        for y in range(MODES_Y):
            ir[0, :, y, :, 0, y] = cx.T
            ir[0, :, y, :, 1, y] = sx.T
            ir[1, :, y, :, 0, y] = -sx.T
            ir[1, :, y, :, 1, y] = cx.T
        ir = ir.reshape(2 * MODES_X * MODES_Y, rows * 2 * MODES_Y)
        ih, il = np_split(ir)
        out.append(np.concatenate([ih, ih, il], 0))
        fold = SCALE * np.where(ky == 0, 1.0, 2.0)[:, None] / (rows * cols)
        inv = np.concatenate([np.cos(ty) * fold, -np.sin(ty) * fold], 0)
        bd = np.zeros((8, 2 * MODES_Y, 8, cols))
        for g in range(8):
            bd[g, :, g, :] = inv
        bh, bl = np_split(bd.reshape(8 * 2 * MODES_Y, 8 * cols))
        out.append(np.concatenate([bh, bh, bl], 0))
        return out


LINEAR = math.sqrt(2.0 / math.pi)
SCALE = (0.044715 * LINEAR) ** (1.0 / 3.0)
SHIFT = LINEAR / SCALE


def scaled_gelu(w):
    return w + w * jnp.tanh(w * (w * w + SHIFT))


def kernel(plan, hid, inn, *refs):
    hbm, out, vm = refs[:22], refs[22], refs[23:45]
    (fields, wbuf, lw, lb, bw, lyb, miw, mib, mow, mob, pw, pb, qm, pm, a1, a2, a3, place, dft, tw, ir, bd) = vm
    (cur, feat, lwm, lwt, vs, pk1, pk2, pk3, u1, u2, u3, r1, r2, r3, lfs, pjs, pbs, wf, win, bcol, wp, lift_b,
     csem, ssem, rsem) = refs[45:]
    lanes = MODES_X * MODES_Y
    ch, rows, cols, nx, ny = plan.ch, plan.rows, plan.cols, plan.nx, plan.ny
    ams, pks, us, recvs = (a1, a2, a3), (pk1, pk2, pk3), (u1, u2, u3), (r1, r2, r3)
    ix, iy = lax.axis_index("gx"), lax.axis_index("gy")

    loads = [pltpu.make_async_copy(h, v, csem.at[n]) for n, (h, v) in enumerate(zip(hbm, vm))]
    for n in (0, 12, 13):
        loads[n].start()
    everyone = plan.everyone
    barrier = pltpu.get_barrier_semaphore()
    for a, b in everyone:
        pl.semaphore_signal(barrier, inc=1, device_id=(lax.rem(ix + a, nx), lax.rem(iy + b, ny)),
                            device_id_type=MESH)
    for n in tuple(range(2, 12)) + (1,) + tuple(range(14, 22)):
        loads[n].start()

    cur[...] = jnp.zeros_like(cur)
    sub = lax.broadcasted_iota(jnp.int32, (rows * FP, cols), 0) % FP
    feat[...] = jnp.where(sub == 4 * ch, 1.0, 0.0).astype(F32)
    for u in us:
        u[...] = jnp.zeros_like(u)
    for n in (0, 12, 13):
        loads[n].wait()
    for c in range(ch):
        cur[pl.ds(c, rows, stride=8), :] = fields[c]

    def pool():
        ch_, cl_ = split(cur[...])
        s = bdot(qm[...], ch_) + bdot(qm[...], cl_)
        sh, sl = split(s)
        start, pstart = 0, 0
        for n, lv in enumerate(plan.lv):
            h, nb, qr, uc = lv["h"], lv["nb"], lv["qrows"], lv["uc"]
            size = h * nb * qr
            lane = lax.broadcasted_iota(jnp.int32, (qr, cols), 1) // uc
            for hy in range(h):
                pmk = pm[pstart:pstart + cols, :]
                pstart += cols
                t = bdot(sh[start:start + size], pmk) + bdot(sl[start:start + size], pmk)
                for hx in range(h):
                    v = t[hx * nb * qr:hx * nb * qr + qr]
                    for b in range(1, nb):
                        o = (hx * nb + b) * qr
                        v = jnp.where(lane == b, t[o:o + qr], v)
                    pks[n][hx * h + hy] = v[0:lv["sr"]]
            start += size

    def send(step):
        for n, slot, a, b in plan.messages:
            lv = plan.lv[n]
            h = lv["h"]
            pltpu.make_async_remote_copy(
                src_ref=pks[n].at[(a % h) * h + b % h, 0:lv["nq"]],
                dst_ref=recvs[n].at[step, slot, 0:lv["nq"]],
                send_sem=ssem.at[step, n], recv_sem=rsem.at[step, n],
                device_id=(lax.rem(ix - a // h + nx, nx), lax.rem(iy - b // h + ny, ny)),
                device_id_type=MESH).start()

    def wait_level(step, sems, n):
        ref = recvs[n].at[step, :, 0:plan.lv[n]["nq"]]
        pltpu.make_async_copy(ref, ref, sems.at[step, n]).wait()

    nf = lw.shape[0]
    hp = functools.partial(jnp.dot, precision=lax.Precision.HIGHEST, preferred_element_type=F32)
    row_of = lambda ref: ref[...].reshape(1, ref.shape[0])
    pool()
    pl.semaphore_wait(barrier, len(everyone))
    send(0)
    for n in range(2, 12):
        loads[n].wait()
    lfs[...] = jnp.zeros_like(lfs)
    lfs[0:nf, :] = lw[...]
    lfs[nf:nf + 1, :] = row_of(lb)
    lf = lfs[...]
    fr = lift_b.shape[0] // 2
    t = jnp.concatenate([jnp.broadcast_to(lf[f:f + 1], (MODES_Y, hid)) for f in range(fr // MODES_Y)], axis=0)
    t = jnp.concatenate([t] * MODES_Y, axis=1)
    rr = lax.broadcasted_iota(jnp.int32, t.shape, 0) % MODES_Y
    ll = lax.broadcasted_iota(jnp.int32, t.shape, 1) // hid
    h, l = split(jnp.where(rr == ll, t, 0.0))
    lift_b[0:fr, :] = h
    lift_b[fr:2 * fr, :] = l
    wb = hp(lf, bw[...])
    wb = wb + jnp.where(lax.broadcasted_iota(jnp.int32, wb.shape, 0) == nf, row_of(lyb), 0.0)
    h, l = split(SCALE * wb.T)
    wf[...] = jnp.concatenate([h, h, l], axis=1)
    pjs[...] = jnp.zeros_like(pjs)
    pjs[0:ch, 0:hid + inn] = jnp.concatenate([pw[...], hp(pw[...], mow[...])], axis=1)
    pj = pjs[:, 0:hid + inn]
    h, l = split((0.5 / SCALE) * pj[:, hid:hid + inn])
    wp[...] = jnp.concatenate(
        [jnp.concatenate([h, h], axis=1), jnp.concatenate([l, jnp.zeros_like(l)], axis=1)], axis=0)
    pbs[...] = jnp.zeros_like(pbs)
    pbs[0:1, 0:inn] = row_of(mib)
    pbs[1:2, 0:ch] = row_of(pb)
    bcol[...] = pbs[...].T
    ob = bcol[0:8, 1:2] + jnp.sum(pj[:, 0:hid] * row_of(mob), axis=1, keepdims=True)
    zero = lambda c: jnp.zeros((8, c), F32)
    h, l = split(jnp.concatenate([0.5 * miw[...].T, (0.5 / SCALE) * pj[:, 0:hid], zero(hid)], axis=0))
    bh, bl = split(jnp.concatenate([SCALE * bcol[0:inn, 0:1], ob, zero(1)], axis=0))
    win[...] = jnp.concatenate([h, h, l, bh, bl, jnp.zeros((inn + 16, 14), BF16)], axis=1)
    for step in range(STEPS):
        if step > 0:
            send(step)
        if step == 0:
            loads[1].wait()
            for m in range(MODES_X):
                w = jnp.concatenate(
                    [wbuf[part, m].reshape(MODES_Y * hid, hid) for part in range(2)], axis=1)
                wh, wl = split(w)
                q = bdot(lift_b[...], jnp.concatenate([wh, wl], axis=1))
                lwm[m] = q[0:fr, 0:2 * hid] + q[fr:, 0:2 * hid] + q[0:fr, 2 * hid:4 * hid]
            for f in range(nf + 1):
                t = lwm[:, f * MODES_Y:(f + 1) * MODES_Y, :].reshape(lanes, 2 * hid).T
                lwt[f] = jnp.concatenate([t[0:hid], t[hid:2 * hid]], axis=1)
            for n in range(14, 22):
                loads[n].wait()
        for r in range(rows):
            feat[r * FP:r * FP + 8, :] = jnp.where(
                lax.broadcasted_iota(jnp.int32, (8, cols), 0) < ch, cur[r * 8:(r + 1) * 8, :],
                feat[r * FP:r * FP + 8, :])
        starts = [sum(len(q["dys"]) for q in plan.lv[:n]) * cols for n in range(len(plan.lv))]
        for n in (0, 1, 2):
            lv = plan.lv[n]
            start = starts[n]
            p, h, sr, ur, uc, nq = (lv[x] for x in ("p", "h", "sr", "ur", "uc", "nq"))
            u = us[n]
            wait_level(step, rsem, n)
            for x, a in enumerate(lv["dxs"]):
                for y, b in enumerate(lv["dys"]):
                    own = (a // h, b // h) == (0, 0)
                    block = pks[n][a * h + b, 0:nq] if own else recvs[n][step, lv["index"][a, b], 0:nq]
                    u[x * sr:x * sr + nq, y * cols:(y + 1) * cols] = block
            uh, ul = split(u[...])
            eh, el = bdot(ams[n][...], uh), bdot(ams[n][...], ul)
            width = len(lv["dys"]) * cols
            row = lax.broadcasted_iota(jnp.int32, (ch * rows, width), 0)
            lane = lax.broadcasted_iota(jnp.int32, (ch * rows, width), 1)
            wpos = row % rows + (lv["r0"] + p * p * ur)
            rho = (row // rows) * ur + wpos % ur
            keep = (lane % cols) // uc == rho // nq
            e = jnp.concatenate(
                [jnp.where(keep, eh, 0.0).astype(BF16), jnp.where(keep, el, 0.0).astype(BF16)], axis=0)
            ctx = bdot(e, place[start:start + width, :])
            ctx = ctx[:ch * rows] + ctx[ch * rows:]
            for c in range(ch):
                feat[pl.ds(ch * (n + 1) + c, rows, stride=FP), :] = ctx[c * rows:(c + 1) * rows]
        fh, fl = split(feat[...])
        z = bdot(jnp.concatenate([fh, fl, fh], axis=1), dft[...])
        parts = []
        for r in range(rows):
            zr = z[r * FP:(r + 1) * FP]
            parts.append(zr[:, 0:2 * lanes] * tw[r:r + 1, :] + zr[:, 2 * lanes:4 * lanes] * tw[rows + r:rows + r + 1, :])
        while len(parts) > 1:
            parts = [a + b for a, b in zip(parts[0::2], parts[1::2])] + ([parts[-1]] if len(parts) % 2 else [])
        hf = parts[0]
        turned = pltpu.roll(hf, lanes, 1)
        first = lax.broadcasted_iota(jnp.int32, hf.shape, 1) < lanes
        f1, f2 = jnp.where(first, hf, turned), jnp.where(first, turned, -hf)
        ga = sum(f1[f:f + 1] * lwt[f] for f in range(nf + 1))
        gb = sum(f2[f:f + 1] * lwt[f] for f in range(nf + 1))
        gh, gl = split(ga + pltpu.roll(gb, lanes, 1))
        ball = bdot(jnp.concatenate([gh, gl, gh], axis=1), ir[...])
        bh, bl = split(ball)
        stack = lambda q: jnp.concatenate(
            [q[:, k * 128:(k + 1) * 128] for k in range(rows // 8)], axis=0)
        bh, bl = stack(bh), stack(bl)
        vs[...] = bdot(jnp.concatenate([bh, bl, bh], axis=1), bd[...])
        ones = jnp.where(lax.broadcasted_iota(jnp.int32, (16, rows * cols), 0) < 2, 1.0, 0.0).astype(BF16)
        for blk in range(rows // rows):
            r0 = blk * rows
            cat = lambda q: jnp.concatenate(
                [q[(r0 + k) * FP:(r0 + k + 1) * FP] for k in range(rows)], axis=1)
            fhc, flc = cat(fh), cat(fl)
            v = jnp.concatenate([vs[(r0 // 8 + j) * hid:(r0 // 8 + j + 1) * hid, :] for j in range(rows // 8)], axis=1)
            v = v + bdot(wf[...], jnp.concatenate([fhc, flc, fhc], axis=0))
            mh, ml = split(scaled_gelu(v))
            t = bdot(win[...], jnp.concatenate([mh, ml, mh, ones], axis=0))
            ih, il = split(scaled_gelu(t[0:inn]))
            o = bdot(wp[...], jnp.concatenate([ih, il], axis=0))
            ov = o[0:8] + o[8:16] + t[inn:inn + 8]
            for k in range(rows):
                cur[(r0 + k) * 8:(r0 + k + 1) * 8, :] += ov[:, k * cols:(k + 1) * cols]
        for n in range(len(plan.lv)):
            wait_level(step, ssem, n)
        if step < STEPS - 1:
            pool()
    for c in range(ch):
        out[c] = cur[pl.ds(c, rows, stride=8), :]


def shards(plan, fields, lift_weight, lift_bias, spectral_weight, bypass_weight, layer_bias, mlp_in_weight,
           mlp_in_bias, mlp_out_weight, mlp_out_bias, project_weight, project_bias):
    ch, rows, cols = fields.shape
    hid = lift_weight.shape[1]
    inn = mlp_in_weight.shape[1]
    consts = [jnp.asarray(c) for c in plan.constants()]
    args = [fields, spectral_weight, lift_weight, lift_bias, bypass_weight, layer_bias, mlp_in_weight,
            mlp_in_bias, mlp_out_weight.T, mlp_out_bias, project_weight.T, project_bias] + consts
    assert len(args) == 22
    scratch = [pltpu.VMEM(a.shape, a.dtype) for a in args]
    fr = round_up(4 * ch + 1, 2) * MODES_Y
    scratch += [
        pltpu.VMEM((rows * 8, cols), F32),
        pltpu.VMEM((rows * FP, cols), F32),
        pltpu.VMEM((MODES_X, fr, 2 * hid), F32),
        pltpu.VMEM((4 * ch + 1, hid, 2 * MODES_X * MODES_Y), F32),
        pltpu.VMEM((rows // 8 * hid, 8 * cols), F32),
    ]
    scratch += [pltpu.VMEM((lv["h"] ** 2, lv["sr"], cols), F32) for lv in plan.lv]
    scratch += [pltpu.VMEM((lv["kpad"], len(lv["dys"]) * cols), F32) for lv in plan.lv]
    scratch += [pltpu.VMEM((STEPS, len(lv["slots"]), lv["sr"], cols), F32) for lv in plan.lv]
    wide = round_up(max(inn, cols), 128)
    scratch += [
        pltpu.VMEM((FP, hid), F32),
        pltpu.VMEM((8, round_up(hid + inn, 128)), F32),
        pltpu.VMEM((8, wide), F32),
        pltpu.VMEM((hid, 3 * FP), BF16),
        pltpu.VMEM((inn + 16, 3 * hid + 16), BF16),
        pltpu.VMEM((wide, 8), F32),
        pltpu.VMEM((16, 2 * inn), BF16),
        pltpu.VMEM((2 * fr, MODES_Y * hid), BF16),
    ]
    scratch += [pltpu.SemaphoreType.DMA((len(args),)), pltpu.SemaphoreType.DMA((STEPS, len(plan.lv))),
                pltpu.SemaphoreType.DMA((STEPS, len(plan.lv)))]
    return pl.pallas_call(
        functools.partial(kernel, plan, hid, inn),
        out_shape=pltpu.VMEM(fields.shape, F32),
        in_specs=[pl.BlockSpec(memory_space=pl.ANY)] * len(args),
        out_specs=pl.BlockSpec(memory_space=pltpu.VMEM),
        scratch_shapes=scratch,
        compiler_params=pltpu.CompilerParams(collective_id=0, has_side_effects=True,
                                             vmem_limit_bytes=60 * 1024 * 1024),
    )(*args)


def solution(mesh):
    nx, ny = mesh.shape["gx"], mesh.shape["gy"]

    def body(fields, *rest):
        plan = Plan(*fields.shape, nx, ny)
        return shards(plan, fields, *rest)

    placed = (P(None, "gx", "gy"),) + (P(),) * 11
    return jax.shard_map(body, mesh=mesh, in_specs=placed, out_specs=P(None, "gx", "gy"), check_vma=False)
```

```python
import functools
import math

import jax
import jax.numpy as jnp
import numpy as np
from jax import lax
from jax.experimental import pallas as pl
from jax.experimental.pallas import tpu as pltpu
from jax.sharding import PartitionSpec as P

MODES_X = 8
MODES_Y = 8
STEPS = 2
LEVELS = (1, 2, 3)
F32 = jnp.float32
BF16 = jnp.bfloat16
FP = 16
MESH = pl.DeviceIdType.MESH


def np_split(a):
    a = np.asarray(a, np.float32)
    hi = a.astype(jnp.bfloat16)
    lo = (a - hi.astype(np.float32)).astype(jnp.bfloat16)
    return hi, lo


def split(x):
    hi = x.astype(BF16)
    lo = (x - hi.astype(F32)).astype(BF16)
    return hi, lo


def bdot(a, b):
    return jnp.dot(a, b, preferred_element_type=F32)


def round_up(n, m):
    return -(-n // m) * m


class Plan:
    def __init__(self, ch, rows, cols, nx, ny):
        self.ch, self.rows, self.cols, self.nx, self.ny = ch, rows, cols, nx, ny
        self.lv = []
        for k in LEVELS:
            p = 2**k
            h = 2 if k == 1 else 1
            nr, nc = rows // p, cols // p
            ur, uc = nr // h, nc // h
            nb = cols // uc
            nq = -(-ch * ur // nb)
            slot_rows = nq if nq in (1, 2, 4) else round_up(nq, 8)
            r0, c0 = -(p - 1) * nr // 2, -(p - 1) * nc // 2
            dxs = sorted({d % (h * nx) for d in range(r0 // ur, (r0 + rows - 1) // ur + 1)})
            dys = sorted({d % (h * ny) for d in range(c0 // uc, (c0 + cols - 1) // uc + 1)})
            slots = [(a, b) for a in dxs for b in dys if (a // h, b // h) != (0, 0)]
            kpad = round_up(len(dxs) * slot_rows, 16)
            self.lv.append(
                dict(p=p, h=h, ur=ur, uc=uc, nb=nb, nq=nq, sr=slot_rows, r0=r0, c0=c0, dxs=dxs, dys=dys,
                     slots=slots, index={q: n for n, q in enumerate(slots)}, kpad=kpad,
                     qrows=round_up(nq, 8))
            )
        def hops(a, b):
            mx = max(nx // 2, 1)
            gx = max(abs(i // mx - (i + a) % nx // mx) + abs(i % mx - (i + a) % nx % mx) for i in range(nx))
            gy = max(abs(j // 2 - (j + b) % ny // 2) for j in range(ny))
            return gx + gy

        def far(m):
            h = self.lv[m[0]]["h"]
            return hops((-(m[2] // h)) % nx, (-(m[3] // h)) % ny)

        self.messages = sorted(
            ((n, slot, a, b) for n, lv in enumerate(self.lv) for slot, (a, b) in enumerate(lv["slots"])),
            key=lambda m: (-far(m), m[0]))
        offs = {(a // lv["h"], b // lv["h"]) for lv in self.lv for a, b in lv["slots"]}
        self.everyone = sorted(offs | {((-a) % nx, (-b) % ny) for a, b in offs}, key=lambda q: (-hops(*q), q))

    def constants(self):
        ch, rows, cols = self.ch, self.rows, self.cols
        q_parts, p_parts, a_parts, place_parts = [], [], [], []
        for lv in self.lv:
            p, h, ur, uc, nb, nq, qr = (lv[x] for x in ("p", "h", "ur", "uc", "nb", "nq", "qrows"))
            q = np.zeros((h, nb, qr, rows * 8), np.float32)
            for hx in range(h):
                for b in range(nb):
                    for t in range(nq):
                        rho = b * nq + t
                        if rho < ch * ur:
                            c, rr = divmod(rho, ur)
                            for u in range(p):
                                q[hx, b, t, ((hx * ur + rr) * p + u) * 8 + c] = 1.0 / p
            q_parts.append(q.reshape(h * nb * qr, rows * 8))
            for hy in range(h):
                pm = np.zeros((cols, cols), np.float32)
                for j in range(uc):
                    for b in range(nb):
                        pm[(hy * uc + j) * p:(hy * uc + j + 1) * p, b * uc + j] = 1.0 / p
                p_parts.append(pm)
            a = np.zeros((ch * rows, lv["kpad"]), np.float32)
            for c in range(ch):
                for w in range(rows):
                    d, rr = divmod(w + lv["r0"], ur)
                    t = (c * ur + rr) % nq
                    a[c * rows + w, lv["dxs"].index(d % (h * self.nx)) * lv["sr"] + t] = 1.0
            a_parts.append(a)
            pl_m = np.zeros((len(lv["dys"]) * cols, cols), np.float32)
            for l in range(cols):
                d, sc = divmod(l + lv["c0"], uc)
                y = lv["dys"].index(d % (h * self.ny))
                for b in range(nb):
                    pl_m[y * cols + b * uc + sc, l] = 1.0
            place_parts.append(pl_m)
        bf = lambda z: np.asarray(z).astype(jnp.bfloat16)
        out = [bf(np.concatenate(q_parts, 0)), bf(np.concatenate(p_parts, 0))]
        out += [bf(a) for a in a_parts]
        out.append(bf(np.concatenate(place_parts, 0)))

        ky = np.arange(MODES_Y)
        mx = np.arange(MODES_X)
        kx = np.where(mx < MODES_X // 2, mx, mx - MODES_X)
        ty = 2 * np.pi * ((np.arange(cols)[None, :] * ky[:, None]) % cols) / cols
        wide = np.concatenate([np.tile(np.cos(ty).T, (1, 2 * MODES_X)), np.tile(np.sin(ty).T, (1, 2 * MODES_X))], 1)
        dh, dl = np_split(wide)
        out.append(np.concatenate([dh, dh, dl], 0))
        tx = 2 * np.pi * ((np.arange(rows)[:, None] * kx[None, :]) % rows) / rows
        cx, sx = np.cos(tx), np.sin(tx)
        cr, sr = np.repeat(cx, MODES_Y, axis=1), np.repeat(sx, MODES_Y, axis=1)
        out.append(np.concatenate([np.concatenate([cr, -sr], 1), np.concatenate([-sr, -cr], 1)], 0).astype(np.float32))
        ir = np.zeros((2, MODES_X, MODES_Y, rows, 2, MODES_Y))
        for y in range(MODES_Y):
            ir[0, :, y, :, 0, y] = cx.T
            ir[0, :, y, :, 1, y] = sx.T
            ir[1, :, y, :, 0, y] = -sx.T
            ir[1, :, y, :, 1, y] = cx.T
        ir = ir.reshape(2 * MODES_X * MODES_Y, rows * 2 * MODES_Y)
        ih, il = np_split(ir)
        out.append(np.concatenate([ih, ih, il], 0))
        fold = SCALE * np.where(ky == 0, 1.0, 2.0)[:, None] / (rows * cols)
        inv = np.concatenate([np.cos(ty) * fold, -np.sin(ty) * fold], 0)
        gr = 64 // (2 * MODES_Y)
        bd = np.zeros((gr, 2 * MODES_Y, gr, cols))
        for g in range(gr):
            bd[g, :, g, :] = inv
        bh, bl = np_split(bd.reshape(gr * 2 * MODES_Y, gr * cols))
        out.append(np.concatenate([bh, bh, bl, np.zeros_like(bl)], 0))
        return out


LINEAR = math.sqrt(2.0 / math.pi)
SCALE = (0.044715 * LINEAR) ** (1.0 / 3.0)
SHIFT = LINEAR / SCALE


def scaled_gelu(w):
    return w + w * jnp.tanh(w * (w * w + SHIFT))


def kernel(plan, hid, inn, *refs):
    hbm, out, vm = refs[:22], refs[22], refs[23:45]
    (fields, wbuf, lw, lb, bw, lyb, miw, mib, mow, mob, pw, pb, qm, pm, a1, a2, a3, place, dft, tw, ir, bd) = vm
    (cur, feat, lwm, lwt, vs, pk1, pk2, pk3, u1, u2, u3, r1, r2, r3, lfs, pjs, pbs, wf, win, bcol, wp, lift_b,
     csem, ssem, rsem) = refs[45:]
    lanes = MODES_X * MODES_Y
    ch, rows, cols, nx, ny = plan.ch, plan.rows, plan.cols, plan.nx, plan.ny
    ams, pks, us, recvs = (a1, a2, a3), (pk1, pk2, pk3), (u1, u2, u3), (r1, r2, r3)
    ix, iy = lax.axis_index("gx"), lax.axis_index("gy")

    loads = [pltpu.make_async_copy(h, v, csem.at[n]) for n, (h, v) in enumerate(zip(hbm, vm))]
    for n in (0, 12, 13):
        loads[n].start()
    everyone = plan.everyone
    barrier = pltpu.get_barrier_semaphore()
    for a, b in everyone:
        pl.semaphore_signal(barrier, inc=1, device_id=(lax.rem(ix + a, nx), lax.rem(iy + b, ny)),
                            device_id_type=MESH)
    for n in tuple(range(2, 12)) + (1,) + tuple(range(14, 22)):
        loads[n].start()

    cur[...] = jnp.zeros_like(cur)
    sub = lax.broadcasted_iota(jnp.int32, (rows * FP, cols), 0) % FP
    feat[...] = jnp.where(sub == 4 * ch, 1.0, 0.0).astype(F32)
    for u in us:
        u[...] = jnp.zeros_like(u)
    for n in (0, 12, 13):
        loads[n].wait()
    for c in range(ch):
        cur[pl.ds(c, rows, stride=8), :] = fields[c]

    def pool():
        ch_, cl_ = split(cur[...])
        s = bdot(qm[...], ch_) + bdot(qm[...], cl_)
        sh, sl = split(s)
        start, pstart = 0, 0
        for n, lv in enumerate(plan.lv):
            h, nb, qr, uc = lv["h"], lv["nb"], lv["qrows"], lv["uc"]
            size = h * nb * qr
            lane = lax.broadcasted_iota(jnp.int32, (qr, cols), 1) // uc
            for hy in range(h):
                pmk = pm[pstart:pstart + cols, :]
                pstart += cols
                t = bdot(sh[start:start + size], pmk) + bdot(sl[start:start + size], pmk)
                for hx in range(h):
                    v = t[hx * nb * qr:hx * nb * qr + qr]
                    for b in range(1, nb):
                        o = (hx * nb + b) * qr
                        v = jnp.where(lane == b, t[o:o + qr], v)
                    pks[n][hx * h + hy] = v[0:lv["sr"]]
            start += size

    def send(step):
        for n, slot, a, b in plan.messages:
            lv = plan.lv[n]
            h = lv["h"]
            pltpu.make_async_remote_copy(
                src_ref=pks[n].at[(a % h) * h + b % h, 0:lv["nq"]],
                dst_ref=recvs[n].at[step, slot, 0:lv["nq"]],
                send_sem=ssem.at[step, n], recv_sem=rsem.at[step, n],
                device_id=(lax.rem(ix - a // h + nx, nx), lax.rem(iy - b // h + ny, ny)),
                device_id_type=MESH).start()

    def wait_level(step, sems, n):
        ref = recvs[n].at[step, :, 0:plan.lv[n]["nq"]]
        pltpu.make_async_copy(ref, ref, sems.at[step, n]).wait()

    nf = lw.shape[0]
    hp = functools.partial(jnp.dot, precision=lax.Precision.HIGHEST, preferred_element_type=F32)
    row_of = lambda ref: ref[...].reshape(1, ref.shape[0])
    pool()
    pl.semaphore_wait(barrier, len(everyone))
    send(0)
    for n in range(2, 12):
        loads[n].wait()
    lfs[...] = jnp.zeros_like(lfs)
    lfs[0:nf, :] = lw[...]
    lfs[nf:nf + 1, :] = row_of(lb)
    lf = lfs[...]
    fr = lift_b.shape[0] // 2
    t = jnp.concatenate([jnp.broadcast_to(lf[f:f + 1], (MODES_Y, hid)) for f in range(fr // MODES_Y)], axis=0)
    t = jnp.concatenate([t] * MODES_Y, axis=1)
    rr = lax.broadcasted_iota(jnp.int32, t.shape, 0) % MODES_Y
    ll = lax.broadcasted_iota(jnp.int32, t.shape, 1) // hid
    h, l = split(jnp.where(rr == ll, t, 0.0))
    lift_b[0:fr, :] = h
    lift_b[fr:2 * fr, :] = l
    wb = hp(lf, bw[...])
    wb = wb + jnp.where(lax.broadcasted_iota(jnp.int32, wb.shape, 0) == nf, row_of(lyb), 0.0)
    h, l = split(SCALE * wb.T)
    wf[...] = jnp.concatenate([h, h, l], axis=1)
    pjs[...] = jnp.zeros_like(pjs)
    pjs[0:ch, 0:hid + inn] = jnp.concatenate([pw[...], hp(pw[...], mow[...])], axis=1)
    pj = pjs[:, 0:hid + inn]
    h, l = split((0.5 / SCALE) * pj[:, hid:hid + inn])
    wp[...] = jnp.concatenate(
        [jnp.concatenate([h, h], axis=1), jnp.concatenate([l, jnp.zeros_like(l)], axis=1)], axis=0)
    pbs[...] = jnp.zeros_like(pbs)
    pbs[0:1, 0:inn] = row_of(mib)
    pbs[1:2, 0:ch] = row_of(pb)
    bcol[...] = pbs[...].T
    ob = bcol[0:8, 1:2] + jnp.sum(pj[:, 0:hid] * row_of(mob), axis=1, keepdims=True)
    zero = lambda c: jnp.zeros((8, c), F32)
    h, l = split(jnp.concatenate([0.5 * miw[...].T, (0.5 / SCALE) * pj[:, 0:hid], zero(hid)], axis=0))
    bh, bl = split(jnp.concatenate([SCALE * bcol[0:inn, 0:1], ob, zero(1)], axis=0))
    win[...] = jnp.concatenate([h, h, l, bh, bl, jnp.zeros((inn + 16, 14), BF16)], axis=1)
    def mix(hi, lo, at):
        if lo is None:
            hi, lo = split(jnp.concatenate(hi, axis=0))
        z = bdot(jnp.concatenate([hi, lo, hi], axis=1), dft[...])
        hf = []
        for c in range(ch):
            zr = z[c * rows:(c + 1) * rows]
            zr = zr[:, 0:2 * lanes] * tw[0:rows, :] + zr[:, 2 * lanes:4 * lanes] * tw[rows:2 * rows, :]
            hf.append(jnp.sum(zr, axis=0, keepdims=True))
        hf = jnp.concatenate(hf, axis=0)
        turned = pltpu.roll(hf, lanes, 1)
        first = lax.broadcasted_iota(jnp.int32, hf.shape, 1) < lanes
        f1, f2 = jnp.where(first, hf, turned), jnp.where(first, turned, -hf)
        return (sum(f1[c:c + 1] * lwt[at + c] for c in range(ch)), sum(f2[c:c + 1] * lwt[at + c] for c in range(ch)))

    for step in range(STEPS):
        if step > 0:
            send(step)
        if step == 0:
            loads[1].wait()
            for m in range(MODES_X):
                w = jnp.concatenate(
                    [wbuf[part, m].reshape(MODES_Y * hid, hid) for part in range(2)], axis=1)
                wh, wl = split(w)
                q = bdot(lift_b[...], jnp.concatenate([wh, wl], axis=1))
                lwm[m] = q[0:fr, 0:2 * hid] + q[fr:, 0:2 * hid] + q[0:fr, 2 * hid:4 * hid]
            for f in range(nf + 1):
                t = lwm[:, f * MODES_Y:(f + 1) * MODES_Y, :].reshape(lanes, 2 * hid).T
                lwt[f] = jnp.concatenate([t[0:hid], t[hid:2 * hid]], axis=1)
            for n in range(14, 22):
                loads[n].wait()
        ga, gb = mix([cur[pl.ds(c, rows, stride=8), :] for c in range(ch)], None, 0)
        at = lax.broadcasted_iota(jnp.int32, (hid, 2 * lanes), 1) % lanes
        ga = ga + jnp.where(at == 0, float(rows * cols), 0.0) * lwt[nf]
        for r in range(rows):
            feat[r * FP:r * FP + 8, :] = jnp.where(
                lax.broadcasted_iota(jnp.int32, (8, cols), 0) < ch, cur[r * 8:(r + 1) * 8, :],
                feat[r * FP:r * FP + 8, :])
        starts = [sum(len(q["dys"]) for q in plan.lv[:n]) * cols for n in range(len(plan.lv))]
        for n in range(len(plan.lv)):
            lv = plan.lv[n]
            start = starts[n]
            if n == 0:
                wait_level(step, rsem, n)
            elif n == 1:
                for later in range(1, len(plan.lv)):
                    wait_level(step, rsem, later)
            p, h, sr, ur, uc, nq = (lv[x] for x in ("p", "h", "sr", "ur", "uc", "nq"))
            u = us[n]
            for x, a in enumerate(lv["dxs"]):
                for y, b in enumerate(lv["dys"]):
                    own = (a // h, b // h) == (0, 0)
                    block = pks[n][a * h + b, 0:nq] if own else recvs[n][step, lv["index"][a, b], 0:nq]
                    u[x * sr:x * sr + nq, y * cols:(y + 1) * cols] = block
            uh, ul = split(u[...])
            eh, el = bdot(ams[n][...], uh), bdot(ams[n][...], ul)
            width = len(lv["dys"]) * cols
            row = lax.broadcasted_iota(jnp.int32, (ch * rows, width), 0)
            lane = lax.broadcasted_iota(jnp.int32, (ch * rows, width), 1)
            wpos = row % rows + (lv["r0"] + p * p * ur)
            rho = (row // rows) * ur + wpos % ur
            keep = (lane % cols) // uc == rho // nq
            e = jnp.concatenate(
                [jnp.where(keep, eh, 0.0).astype(BF16), jnp.where(keep, el, 0.0).astype(BF16)], axis=0)
            ctx = bdot(e, place[start:start + width, :])
            ma, mb = mix(ctx[:ch * rows].astype(BF16), ctx[ch * rows:].astype(BF16), ch * (n + 1))
            ga, gb = ga + ma, gb + mb
            ctx = ctx[:ch * rows] + ctx[ch * rows:]
            for c in range(ch):
                feat[pl.ds(ch * (n + 1) + c, rows, stride=FP), :] = ctx[c * rows:(c + 1) * rows]
        fh, fl = split(feat[...])
        gh, gl = split(ga + pltpu.roll(gb, lanes, 1))
        ball = bdot(jnp.concatenate([gh, gl, gh], axis=1), ir[...])
        low = lax.broadcasted_iota(jnp.int32, (hid, 128), 1) < 64
        pieces = []
        for k in range(ball.shape[1] // 128):
            p = ball[:, k * 128:(k + 1) * 128]
            q = pltpu.roll(p, 64, 1)
            for a, b in ((p, q), (q, p)):
                rest = b - b.astype(BF16).astype(F32)
                pieces.append(jnp.concatenate([jnp.where(low, a, rest).astype(BF16), a.astype(BF16)], axis=1))
        vs[...] = bdot(jnp.concatenate(pieces, axis=0), bd[...])
        ones = jnp.where(lax.broadcasted_iota(jnp.int32, (16, rows * cols), 0) < 2, 1.0, 0.0).astype(BF16)
        for blk in range(rows // rows):
            r0 = blk * rows
            cat = lambda q: jnp.concatenate(
                [q[(r0 + k) * FP:(r0 + k + 1) * FP] for k in range(rows)], axis=1)
            fhc, flc = cat(fh), cat(fl)
            v = jnp.concatenate([vs[j * hid:(j + 1) * hid, :] for j in range(vs.shape[0] // hid)], axis=1)
            v = v + bdot(wf[...], jnp.concatenate([fhc, flc, fhc], axis=0))
            mh, ml = split(scaled_gelu(v))
            t = bdot(win[...], jnp.concatenate([mh, ml, mh, ones], axis=0))
            ih, il = split(scaled_gelu(t[0:inn]))
            o = bdot(wp[...], jnp.concatenate([ih, il], axis=0))
            ov = o[0:8] + o[8:16] + t[inn:inn + 8]
            for k in range(rows):
                cur[(r0 + k) * 8:(r0 + k + 1) * 8, :] += ov[:, k * cols:(k + 1) * cols]
        for n in range(len(plan.lv)):
            wait_level(step, ssem, n)
        if step < STEPS - 1:
            pool()
    for c in range(ch):
        out[c] = cur[pl.ds(c, rows, stride=8), :]


def shards(plan, fields, lift_weight, lift_bias, spectral_weight, bypass_weight, layer_bias, mlp_in_weight,
           mlp_in_bias, mlp_out_weight, mlp_out_bias, project_weight, project_bias):
    ch, rows, cols = fields.shape
    hid = lift_weight.shape[1]
    inn = mlp_in_weight.shape[1]
    consts = [jnp.asarray(c) for c in plan.constants()]
    args = [fields, spectral_weight, lift_weight, lift_bias, bypass_weight, layer_bias, mlp_in_weight,
            mlp_in_bias, mlp_out_weight.T, mlp_out_bias, project_weight.T, project_bias] + consts
    assert len(args) == 22
    scratch = [pltpu.VMEM(a.shape, a.dtype) for a in args]
    fr = round_up(4 * ch + 1, 2) * MODES_Y
    scratch += [
        pltpu.VMEM((rows * 8, cols), F32),
        pltpu.VMEM((rows * FP, cols), F32),
        pltpu.VMEM((MODES_X, fr, 2 * hid), F32),
        pltpu.VMEM((4 * ch + 1, hid, 2 * MODES_X * MODES_Y), F32),
        pltpu.VMEM((rows * MODES_Y // 32 * hid, 32 // MODES_Y * cols), F32),
    ]
    scratch += [pltpu.VMEM((lv["h"] ** 2, lv["sr"], cols), F32) for lv in plan.lv]
    scratch += [pltpu.VMEM((lv["kpad"], len(lv["dys"]) * cols), F32) for lv in plan.lv]
    scratch += [pltpu.VMEM((STEPS, len(lv["slots"]), lv["sr"], cols), F32) for lv in plan.lv]
    wide = round_up(max(inn, cols), 128)
    scratch += [
        pltpu.VMEM((FP, hid), F32),
        pltpu.VMEM((8, round_up(hid + inn, 128)), F32),
        pltpu.VMEM((8, wide), F32),
        pltpu.VMEM((hid, 3 * FP), BF16),
        pltpu.VMEM((inn + 16, 3 * hid + 16), BF16),
        pltpu.VMEM((wide, 8), F32),
        pltpu.VMEM((16, 2 * inn), BF16),
        pltpu.VMEM((2 * fr, MODES_Y * hid), BF16),
    ]
    scratch += [pltpu.SemaphoreType.DMA((len(args),)), pltpu.SemaphoreType.DMA((STEPS, len(plan.lv))),
                pltpu.SemaphoreType.DMA((STEPS, len(plan.lv)))]
    return pl.pallas_call(
        functools.partial(kernel, plan, hid, inn),
        out_shape=pltpu.VMEM(fields.shape, F32),
        in_specs=[pl.BlockSpec(memory_space=pl.ANY)] * len(args),
        out_specs=pl.BlockSpec(memory_space=pltpu.VMEM),
        scratch_shapes=scratch,
        compiler_params=pltpu.CompilerParams(collective_id=0, has_side_effects=True,
                                             vmem_limit_bytes=60 * 1024 * 1024),
    )(*args)


def solution(mesh):
    nx, ny = mesh.shape["gx"], mesh.shape["gy"]

    def body(fields, *rest):
        plan = Plan(*fields.shape, nx, ny)
        return shards(plan, fields, *rest)

    placed = (P(None, "gx", "gy"),) + (P(),) * 11
    return jax.shard_map(body, mesh=mesh, in_specs=placed, out_specs=P(None, "gx", "gy"), check_vma=False)
```

```python
import functools
import math

import jax
import jax.numpy as jnp
import numpy as np
from jax import lax
from jax.experimental import pallas as pl
from jax.experimental.pallas import tpu as pltpu
from jax.sharding import PartitionSpec as P

MODES_X = 8
MODES_Y = 8
STEPS = 2
LEVELS = (1, 2, 3)
F32 = jnp.float32
BF16 = jnp.bfloat16
FP = 16
MESH = pl.DeviceIdType.MESH


def np_split(a):
    a = np.asarray(a, np.float32)
    hi = a.astype(jnp.bfloat16)
    lo = (a - hi.astype(np.float32)).astype(jnp.bfloat16)
    return hi, lo


def split(x):
    hi = x.astype(BF16)
    lo = (x - hi.astype(F32)).astype(BF16)
    return hi, lo


def bdot(a, b):
    return jnp.dot(a, b, preferred_element_type=F32)


def round_up(n, m):
    return -(-n // m) * m


class Plan:
    def __init__(self, ch, rows, cols, nx, ny):
        self.ch, self.rows, self.cols, self.nx, self.ny = ch, rows, cols, nx, ny
        self.lv = []
        for k in LEVELS:
            p = 2**k
            h = 2 if k == 1 else 1
            nr, nc = rows // p, cols // p
            ur, uc = nr // h, nc // h
            nb = cols // uc
            nq = -(-ch * ur // nb)
            slot_rows = nq if nq in (1, 2, 4) else round_up(nq, 8)
            r0, c0 = -(p - 1) * nr // 2, -(p - 1) * nc // 2
            dxs = sorted({d % (h * nx) for d in range(r0 // ur, (r0 + rows - 1) // ur + 1)})
            dys = sorted({d % (h * ny) for d in range(c0 // uc, (c0 + cols - 1) // uc + 1)})
            slots = [(a, b) for a in dxs for b in dys if (a // h, b // h) != (0, 0)]
            kpad = round_up(len(dxs) * slot_rows, 8)
            origin = []
            for b in range(-(-ch * ur // nq)):
                for i in range(kpad):
                    x, t = divmod(i, slot_rows)
                    c, rr = divmod(b * nq + t, ur)
                    ok = x < len(dxs) and t < nq and c < ch
                    ws = [w for w in range(rows) if ok and (w + r0) % ur == rr
                          and (w + r0) // ur % (h * nx) == dxs[x]]
                    origin.append((c, ws) if ok else (None, []))
            self.lv.append(
                dict(p=p, h=h, ur=ur, uc=uc, nb=nb, nq=nq, sr=slot_rows, r0=r0, c0=c0, dxs=dxs, dys=dys,
                     slots=slots, index={q: n for n, q in enumerate(slots)}, kpad=kpad, origin=origin,
                     qrows=round_up(nq, 8))
            )
        def hops(a, b):
            mx = max(nx // 2, 1)
            gx = max(abs(i // mx - (i + a) % nx // mx) + abs(i % mx - (i + a) % nx % mx) for i in range(nx))
            gy = max(abs(j // 2 - (j + b) % ny // 2) for j in range(ny))
            return gx + gy

        def far(m):
            h = self.lv[m[0]]["h"]
            return hops((-(m[2] // h)) % nx, (-(m[3] // h)) % ny)

        self.messages = sorted(
            ((n, slot, a, b) for n, lv in enumerate(self.lv) for slot, (a, b) in enumerate(lv["slots"])),
            key=lambda m: (-far(m), m[0]))
        offs = {(a // lv["h"], b // lv["h"]) for lv in self.lv for a, b in lv["slots"]}
        self.everyone = sorted(offs | {((-a) % nx, (-b) % ny) for a, b in offs}, key=lambda q: (-hops(*q), q))

    def constants(self):
        ch, rows, cols = self.ch, self.rows, self.cols
        q_parts, p_parts = [], []
        for lv in self.lv:
            p, h, ur, uc, nb, nq, qr = (lv[x] for x in ("p", "h", "ur", "uc", "nb", "nq", "qrows"))
            q = np.zeros((h, nb, qr, rows * 8), np.float32)
            for hx in range(h):
                for b in range(nb):
                    for t in range(nq):
                        rho = b * nq + t
                        if rho < ch * ur:
                            c, rr = divmod(rho, ur)
                            for u in range(p):
                                q[hx, b, t, ((hx * ur + rr) * p + u) * 8 + c] = 1.0 / p
            q_parts.append(q.reshape(h * nb * qr, rows * 8))
            for hy in range(h):
                pm = np.zeros((cols, cols), np.float32)
                for j in range(uc):
                    for b in range(nb):
                        pm[(hy * uc + j) * p:(hy * uc + j + 1) * p, b * uc + j] = 1.0 / p
                p_parts.append(pm)
        bf = lambda z: np.asarray(z).astype(jnp.bfloat16)
        out = [bf(np.concatenate(q_parts, 0)), bf(np.concatenate(p_parts, 0))]

        ky = np.arange(MODES_Y)
        mx = np.arange(MODES_X)
        kx = np.where(mx < MODES_X // 2, mx, mx - MODES_X)
        ty = 2 * np.pi * ((np.arange(cols)[None, :] * ky[:, None]) % cols) / cols
        wide = np.concatenate([np.tile(np.cos(ty).T, (1, 2 * MODES_X)), np.tile(np.sin(ty).T, (1, 2 * MODES_X))], 1)
        dh, dl = np_split(wide)
        out.append(np.concatenate([dh, dh, dl], 0))
        tx = 2 * np.pi * ((np.arange(rows)[:, None] * kx[None, :]) % rows) / rows
        cx, sx = np.cos(tx), np.sin(tx)
        cr, sr = np.repeat(cx, MODES_Y, axis=1), np.repeat(sx, MODES_Y, axis=1)
        turns = np.concatenate([cr, -sr, -sr, -cr], 1).astype(np.float32)
        out.append(turns)
        out.append(np.stack([turns[ws].sum(0) for lv in self.lv for _, ws in lv["origin"]]))
        ir = np.zeros((2, MODES_X, MODES_Y, rows, 2, MODES_Y))
        for y in range(MODES_Y):
            ir[0, :, y, :, 0, y] = cx.T
            ir[0, :, y, :, 1, y] = sx.T
            ir[1, :, y, :, 0, y] = -sx.T
            ir[1, :, y, :, 1, y] = cx.T
        ir = ir.reshape(2 * MODES_X * MODES_Y, rows * 2 * MODES_Y)
        ih, il = np_split(ir)
        out.append(np.concatenate([ih, ih, il], 0))
        fold = SCALE * np.where(ky == 0, 1.0, 2.0)[:, None] / (rows * cols)
        inv = np.concatenate([np.cos(ty) * fold, -np.sin(ty) * fold], 0)
        gr = 64 // (2 * MODES_Y)
        bd = np.zeros((gr, 2 * MODES_Y, gr, cols))
        for g in range(gr):
            bd[g, :, g, :] = inv
        bh, bl = np_split(bd.reshape(gr * 2 * MODES_Y, gr * cols))
        out.append(np.concatenate([bh, bh, bl, np.zeros_like(bl)], 0))
        return out


LINEAR = math.sqrt(2.0 / math.pi)
SCALE = (0.044715 * LINEAR) ** (1.0 / 3.0)
SHIFT = LINEAR / SCALE


def scaled_gelu(w):
    return w + w * jnp.tanh(w * (w * w + SHIFT))


def kernel(plan, hid, inn, *refs):
    hbm, out, vm = refs[:19], refs[19], refs[20:39]
    (fields, wbuf, lw, lb, bw, lyb, miw, mib, mow, mob, pw, pb, qm, pm, dft, tw, tab, ir, bd) = vm
    (cur, feat, lwm, lwt, vs, pk1, pk2, pk3, u1, u2, u3, r1, r2, r3, lfs, pjs, pbs, wf, win, bcol, wp, lift_b,
     csem, ssem, rsem) = refs[39:]
    lanes = MODES_X * MODES_Y
    ch, rows, cols, nx, ny = plan.ch, plan.rows, plan.cols, plan.nx, plan.ny
    pks, us, recvs = (pk1, pk2, pk3), (u1, u2, u3), (r1, r2, r3)
    ix, iy = lax.axis_index("gx"), lax.axis_index("gy")

    loads = [pltpu.make_async_copy(h, v, csem.at[n]) for n, (h, v) in enumerate(zip(hbm, vm))]
    for n in (0, 12, 13):
        loads[n].start()
    everyone = plan.everyone
    barrier = pltpu.get_barrier_semaphore()
    for a, b in everyone:
        pl.semaphore_signal(barrier, inc=1, device_id=(lax.rem(ix + a, nx), lax.rem(iy + b, ny)),
                            device_id_type=MESH)
    for n in tuple(range(2, 12)) + (1,) + tuple(range(14, 19)):
        loads[n].start()

    cur[...] = jnp.zeros_like(cur)
    sub = lax.broadcasted_iota(jnp.int32, (rows * FP, cols), 0) % FP
    feat[...] = jnp.where(sub == 4 * ch, 1.0, 0.0).astype(F32)
    for u in us:
        u[...] = jnp.zeros_like(u)
    for n in (0, 12, 13):
        loads[n].wait()
    for c in range(ch):
        cur[pl.ds(c, rows, stride=8), :] = fields[c]

    def pool():
        ch_, cl_ = split(cur[...])
        s = bdot(qm[...], ch_) + bdot(qm[...], cl_)
        sh, sl = split(s)
        start, pstart = 0, 0
        for n, lv in enumerate(plan.lv):
            h, nb, qr, uc = lv["h"], lv["nb"], lv["qrows"], lv["uc"]
            size = h * nb * qr
            lane = lax.broadcasted_iota(jnp.int32, (qr, cols), 1) // uc
            for hy in range(h):
                pmk = pm[pstart:pstart + cols, :]
                pstart += cols
                t = bdot(sh[start:start + size], pmk) + bdot(sl[start:start + size], pmk)
                for hx in range(h):
                    v = t[hx * nb * qr:hx * nb * qr + qr]
                    for b in range(1, nb):
                        o = (hx * nb + b) * qr
                        v = jnp.where(lane == b, t[o:o + qr], v)
                    pks[n][hx * h + hy] = v[0:lv["sr"]]
            start += size

    def send(step):
        for n, slot, a, b in plan.messages:
            lv = plan.lv[n]
            h = lv["h"]
            pltpu.make_async_remote_copy(
                src_ref=pks[n].at[(a % h) * h + b % h, 0:lv["nq"]],
                dst_ref=recvs[n].at[step, slot, 0:lv["nq"]],
                send_sem=ssem.at[step, n], recv_sem=rsem.at[step, n],
                device_id=(lax.rem(ix - a // h + nx, nx), lax.rem(iy - b // h + ny, ny)),
                device_id_type=MESH).start()

    def wait_level(step, sems, n):
        ref = recvs[n].at[step, :, 0:plan.lv[n]["nq"]]
        pltpu.make_async_copy(ref, ref, sems.at[step, n]).wait()

    nf = lw.shape[0]
    hp = functools.partial(jnp.dot, precision=lax.Precision.HIGHEST, preferred_element_type=F32)
    row_of = lambda ref: ref[...].reshape(1, ref.shape[0])
    pool()
    pl.semaphore_wait(barrier, len(everyone))
    send(0)
    for n in range(2, 12):
        loads[n].wait()
    lfs[...] = jnp.zeros_like(lfs)
    lfs[0:nf, :] = lw[...]
    lfs[nf:nf + 1, :] = row_of(lb)
    lf = lfs[...]
    fr = lift_b.shape[0] // 2
    t = jnp.concatenate([jnp.broadcast_to(lf[f:f + 1], (MODES_Y, hid)) for f in range(fr // MODES_Y)], axis=0)
    t = jnp.concatenate([t] * MODES_Y, axis=1)
    rr = lax.broadcasted_iota(jnp.int32, t.shape, 0) % MODES_Y
    ll = lax.broadcasted_iota(jnp.int32, t.shape, 1) // hid
    h, l = split(jnp.where(rr == ll, t, 0.0))
    lift_b[0:fr, :] = h
    lift_b[fr:2 * fr, :] = l
    wb = hp(lf, bw[...])
    wb = wb + jnp.where(lax.broadcasted_iota(jnp.int32, wb.shape, 0) == nf, row_of(lyb), 0.0)
    h, l = split(SCALE * wb.T)
    wf[...] = jnp.concatenate([h, h, l], axis=1)
    pjs[...] = jnp.zeros_like(pjs)
    pjs[0:ch, 0:hid + inn] = jnp.concatenate([pw[...], hp(pw[...], mow[...])], axis=1)
    pj = pjs[:, 0:hid + inn]
    h, l = split((0.5 / SCALE) * pj[:, hid:hid + inn])
    wp[...] = jnp.concatenate(
        [jnp.concatenate([h, h], axis=1), jnp.concatenate([l, jnp.zeros_like(l)], axis=1)], axis=0)
    pbs[...] = jnp.zeros_like(pbs)
    pbs[0:1, 0:inn] = row_of(mib)
    pbs[1:2, 0:ch] = row_of(pb)
    bcol[...] = pbs[...].T
    ob = bcol[0:8, 1:2] + jnp.sum(pj[:, 0:hid] * row_of(mob), axis=1, keepdims=True)
    zero = lambda c: jnp.zeros((8, c), F32)
    h, l = split(jnp.concatenate([0.5 * miw[...].T, (0.5 / SCALE) * pj[:, 0:hid], zero(hid)], axis=0))
    bh, bl = split(jnp.concatenate([SCALE * bcol[0:inn, 0:1], ob, zero(1)], axis=0))
    win[...] = jnp.concatenate([h, h, l, bh, bl, jnp.zeros((inn + 16, 14), BF16)], axis=1)
    def transform(x):
        hi, lo = split(x)
        return bdot(jnp.concatenate([hi, lo, hi], axis=1), dft[...])

    def turn(z, t):
        return z[:, 0:2 * lanes] * t[:, 0:2 * lanes] + z[:, 2 * lanes:4 * lanes] * t[:, 2 * lanes:4 * lanes]

    def add_up(p, owners):
        sums = [None] * ch
        for v in range(0, len(owners), 8):
            own = owners[v:v + 8]
            for c in range(ch):
                at = [i for i in range(8) if own[i] == c]
                if at:
                    q = p[v:v + 8]
                    if any(o not in (None, c) for o in own):
                        assert at == list(range(at[0], at[-1] + 1))
                        i = lax.broadcasted_iota(jnp.int32, q.shape, 0)
                        q = jnp.where((i >= at[0]) & (i <= at[-1]), q, 0.0)
                    sums[c] = q if sums[c] is None else sums[c] + q
        return [jnp.sum(q, axis=0, keepdims=True) for q in sums]

    def mix(hf, at):
        hf = jnp.concatenate(hf, axis=0)
        turned = pltpu.roll(hf, lanes, 1)
        first = lax.broadcasted_iota(jnp.int32, hf.shape, 1) < lanes
        f1, f2 = jnp.where(first, hf, turned), jnp.where(first, turned, -hf)
        return (sum(f1[c:c + 1] * lwt[at + c] for c in range(ch)), sum(f2[c:c + 1] * lwt[at + c] for c in range(ch)))

    for step in range(STEPS):
        if step > 0:
            send(step)
        if step == 0:
            loads[1].wait()
            for m in range(MODES_X):
                w = jnp.concatenate(
                    [wbuf[part, m].reshape(MODES_Y * hid, hid) for part in range(2)], axis=1)
                wh, wl = split(w)
                q = bdot(lift_b[...], jnp.concatenate([wh, wl], axis=1))
                lwm[m] = q[0:fr, 0:2 * hid] + q[fr:, 0:2 * hid] + q[0:fr, 2 * hid:4 * hid]
            for f in range(nf + 1):
                t = lwm[:, f * MODES_Y:(f + 1) * MODES_Y, :].reshape(lanes, 2 * hid).T
                lwt[f] = jnp.concatenate([t[0:hid], t[hid:2 * hid]], axis=1)
            for n in range(14, 19):
                loads[n].wait()
        z = transform(jnp.concatenate([cur[pl.ds(c, rows, stride=8), :] for c in range(ch)], axis=0))
        z = turn(z, jnp.concatenate([tw[...]] * ch, axis=0))
        ga, gb = mix(add_up(z, [c for c in range(ch) for _ in range(rows)]), 0)
        at = lax.broadcasted_iota(jnp.int32, (hid, 2 * lanes), 1) % lanes
        ga = ga + jnp.where(at == 0, float(rows * cols), 0.0) * lwt[nf]
        for r in range(rows):
            feat[r * FP:r * FP + 8, :] = jnp.where(
                lax.broadcasted_iota(jnp.int32, (8, cols), 0) < ch, cur[r * 8:(r + 1) * 8, :],
                feat[r * FP:r * FP + 8, :])
        starts = [sum(len(q["origin"]) for q in plan.lv[:n]) for n in range(len(plan.lv))]
        for n in range(len(plan.lv)):
            lv = plan.lv[n]
            start = starts[n]
            if n == 0:
                wait_level(step, rsem, n)
            elif n == 1:
                for later in range(1, len(plan.lv)):
                    wait_level(step, rsem, later)
            p, h, sr, ur, uc, nq = (lv[x] for x in ("p", "h", "sr", "ur", "uc", "nq"))
            u = us[n]
            for x, a in enumerate(lv["dxs"]):
                for y, b in enumerate(lv["dys"]):
                    own = (a // h, b // h) == (0, 0)
                    block = pks[n][a * h + b, 0:nq] if own else recvs[n][step, lv["index"][a, b], 0:nq]
                    u[x * sr:x * sr + nq, y * cols:(y + 1) * cols] = block
            groups = []
            kpad, nb, uc, origin = lv["kpad"], lv["nb"], lv["uc"], lv["origin"]
            lane = lax.broadcasted_iota(jnp.int32, (kpad, cols), 1)
            for b in range(len(origin) // kpad):
                for d in range(lv["c0"] // uc, (lv["c0"] + cols - 1) // uc + 1):
                    y = lv["dys"].index(d % (h * ny))
                    block = u[:, y * cols:(y + 1) * cols]
                    shift = ((d - b) * uc - lv["c0"]) % cols
                    block = pltpu.roll(block, shift, 1) if shift else block
                    l0 = d * uc - lv["c0"]
                    acc = block if l0 <= 0 else jnp.where(lane >= l0, block, acc)
                groups.append(acc)
            ctx = jnp.concatenate(groups, axis=0)
            z = turn(transform(ctx), tab[start:start + len(origin), :])
            ma, mb = mix(add_up(z, [c for c, _ in origin]), ch * (n + 1))
            ga, gb = ga + ma, gb + mb
            for i, (c, ws) in enumerate(origin):
                for w in ws:
                    k = w * FP + ch * (n + 1) + c
                    feat[k:k + 1, :] = ctx[i:i + 1]
        fh, fl = split(feat[...])
        gh, gl = split(ga + pltpu.roll(gb, lanes, 1))
        ball = bdot(jnp.concatenate([gh, gl, gh], axis=1), ir[...])
        low = lax.broadcasted_iota(jnp.int32, (hid, 128), 1) < 64
        pieces = []
        for k in range(ball.shape[1] // 128):
            p = ball[:, k * 128:(k + 1) * 128]
            q = pltpu.roll(p, 64, 1)
            for a, b in ((p, q), (q, p)):
                rest = b - b.astype(BF16).astype(F32)
                pieces.append(jnp.concatenate([jnp.where(low, a, rest).astype(BF16), a.astype(BF16)], axis=1))
        vs[...] = bdot(jnp.concatenate(pieces, axis=0), bd[...])
        ones = jnp.where(lax.broadcasted_iota(jnp.int32, (16, rows * cols), 0) < 2, 1.0, 0.0).astype(BF16)
        for blk in range(rows // rows):
            r0 = blk * rows
            cat = lambda q: jnp.concatenate(
                [q[(r0 + k) * FP:(r0 + k + 1) * FP] for k in range(rows)], axis=1)
            fhc, flc = cat(fh), cat(fl)
            v = jnp.concatenate([vs[j * hid:(j + 1) * hid, :] for j in range(vs.shape[0] // hid)], axis=1)
            v = v + bdot(wf[...], jnp.concatenate([fhc, flc, fhc], axis=0))
            mh, ml = split(scaled_gelu(v))
            t = bdot(win[...], jnp.concatenate([mh, ml, mh, ones], axis=0))
            ih, il = split(scaled_gelu(t[0:inn]))
            o = bdot(wp[...], jnp.concatenate([ih, il], axis=0))
            ov = o[0:8] + o[8:16] + t[inn:inn + 8]
            for k in range(rows):
                cur[(r0 + k) * 8:(r0 + k + 1) * 8, :] += ov[:, k * cols:(k + 1) * cols]
        for n in range(len(plan.lv)):
            wait_level(step, ssem, n)
        if step < STEPS - 1:
            pool()
    for c in range(ch):
        out[c] = cur[pl.ds(c, rows, stride=8), :]


def shards(plan, fields, lift_weight, lift_bias, spectral_weight, bypass_weight, layer_bias, mlp_in_weight,
           mlp_in_bias, mlp_out_weight, mlp_out_bias, project_weight, project_bias):
    ch, rows, cols = fields.shape
    hid = lift_weight.shape[1]
    inn = mlp_in_weight.shape[1]
    consts = [jnp.asarray(c) for c in plan.constants()]
    args = [fields, spectral_weight, lift_weight, lift_bias, bypass_weight, layer_bias, mlp_in_weight,
            mlp_in_bias, mlp_out_weight.T, mlp_out_bias, project_weight.T, project_bias] + consts
    assert len(args) == 19
    scratch = [pltpu.VMEM(a.shape, a.dtype) for a in args]
    fr = round_up(4 * ch + 1, 2) * MODES_Y
    scratch += [
        pltpu.VMEM((rows * 8, cols), F32),
        pltpu.VMEM((rows * FP, cols), F32),
        pltpu.VMEM((MODES_X, fr, 2 * hid), F32),
        pltpu.VMEM((4 * ch + 1, hid, 2 * MODES_X * MODES_Y), F32),
        pltpu.VMEM((rows * MODES_Y // 32 * hid, 32 // MODES_Y * cols), F32),
    ]
    scratch += [pltpu.VMEM((lv["h"] ** 2, lv["sr"], cols), F32) for lv in plan.lv]
    scratch += [pltpu.VMEM((lv["kpad"], len(lv["dys"]) * cols), F32) for lv in plan.lv]
    scratch += [pltpu.VMEM((STEPS, len(lv["slots"]), lv["sr"], cols), F32) for lv in plan.lv]
    wide = round_up(max(inn, cols), 128)
    scratch += [
        pltpu.VMEM((FP, hid), F32),
        pltpu.VMEM((8, round_up(hid + inn, 128)), F32),
        pltpu.VMEM((8, wide), F32),
        pltpu.VMEM((hid, 3 * FP), BF16),
        pltpu.VMEM((inn + 16, 3 * hid + 16), BF16),
        pltpu.VMEM((wide, 8), F32),
        pltpu.VMEM((16, 2 * inn), BF16),
        pltpu.VMEM((2 * fr, MODES_Y * hid), BF16),
    ]
    scratch += [pltpu.SemaphoreType.DMA((len(args),)), pltpu.SemaphoreType.DMA((STEPS, len(plan.lv))),
                pltpu.SemaphoreType.DMA((STEPS, len(plan.lv)))]
    return pl.pallas_call(
        functools.partial(kernel, plan, hid, inn),
        out_shape=pltpu.VMEM(fields.shape, F32),
        in_specs=[pl.BlockSpec(memory_space=pl.ANY)] * len(args),
        out_specs=pl.BlockSpec(memory_space=pltpu.VMEM),
        scratch_shapes=scratch,
        compiler_params=pltpu.CompilerParams(collective_id=0, has_side_effects=True,
                                             vmem_limit_bytes=60 * 1024 * 1024),
    )(*args)


def solution(mesh):
    nx, ny = mesh.shape["gx"], mesh.shape["gy"]

    def body(fields, *rest):
        plan = Plan(*fields.shape, nx, ny)
        return shards(plan, fields, *rest)

    placed = (P(None, "gx", "gy"),) + (P(),) * 11
    return jax.shard_map(body, mesh=mesh, in_specs=placed, out_specs=P(None, "gx", "gy"), check_vma=False)
```

```python
import functools
import math

import jax
import jax.numpy as jnp
import numpy as np
from jax import lax
from jax.experimental import pallas as pl
from jax.experimental.pallas import tpu as pltpu
from jax.sharding import PartitionSpec as P

MODES_X = 8
MODES_Y = 8
STEPS = 2
LEVELS = (1, 2, 3)
F32 = jnp.float32
BF16 = jnp.bfloat16
FP = 16
MESH = pl.DeviceIdType.MESH


def np_split(a):
    a = np.asarray(a, np.float32)
    hi = a.astype(jnp.bfloat16)
    lo = (a - hi.astype(np.float32)).astype(jnp.bfloat16)
    return hi, lo


def split(x):
    hi = x.astype(BF16)
    lo = (x - hi.astype(F32)).astype(BF16)
    return hi, lo


def bdot(a, b):
    return jnp.dot(a, b, preferred_element_type=F32)


def round_up(n, m):
    return -(-n // m) * m


class Plan:
    def __init__(self, ch, rows, cols, nx, ny):
        self.ch, self.rows, self.cols, self.nx, self.ny = ch, rows, cols, nx, ny
        self.lv = []
        for k in LEVELS:
            p = 2**k
            h = 2 if k == 1 else 1
            nr, nc = rows // p, cols // p
            ur, uc = nr // h, nc // h
            nb = cols // uc
            nq = -(-ch * ur // nb)
            slot_rows = nq if nq in (1, 2, 4) else round_up(nq, 8)
            r0, c0 = -(p - 1) * nr // 2, -(p - 1) * nc // 2
            dxs = sorted({d % (h * nx) for d in range(r0 // ur, (r0 + rows - 1) // ur + 1)})
            dys = sorted({d % (h * ny) for d in range(c0 // uc, (c0 + cols - 1) // uc + 1)})
            slots = [(a, b) for a in dxs for b in dys if (a // h, b // h) != (0, 0)]
            kpad = round_up(len(dxs) * slot_rows, 8)
            origin = []
            for b in range(-(-ch * ur // nq)):
                for i in range(kpad):
                    x, t = divmod(i, slot_rows)
                    c, rr = divmod(b * nq + t, ur)
                    ok = x < len(dxs) and t < nq and c < ch
                    ws = [w for w in range(rows) if ok and (w + r0) % ur == rr
                          and (w + r0) // ur % (h * nx) == dxs[x]]
                    origin.append((c, ws) if ok else (None, []))
            self.lv.append(
                dict(p=p, h=h, ur=ur, uc=uc, nb=nb, nq=nq, sr=slot_rows, r0=r0, c0=c0, dxs=dxs, dys=dys,
                     slots=slots, index={q: n for n, q in enumerate(slots)}, kpad=kpad, origin=origin,
                     qrows=round_up(nq, 8))
            )
        one, two, three = self.lv
        assert two["h"] == three["h"] == 1 and two["nq"] + three["nq"] <= 8
        three["slots"] = [q for q in three["slots"] if q not in two["index"]]
        three["index"] = {q: n for n, q in enumerate(three["slots"])}
        one.update(at=0, send=one["nq"])
        two.update(at=three["nq"], send=two["nq"] + three["nq"])
        three.update(at=0, send=three["nq"])

        def hops(a, b):
            mx = max(nx // 2, 1)
            gx = max(abs(i // mx - (i + a) % nx // mx) + abs(i % mx - (i + a) % nx % mx) for i in range(nx))
            gy = max(abs(j // 2 - (j + b) % ny // 2) for j in range(ny))
            return gx + gy

        def far(m):
            h = self.lv[m[0]]["h"]
            return hops((-(m[2] // h)) % nx, (-(m[3] // h)) % ny)

        self.messages = sorted(
            ((n, slot, a, b) for n, lv in enumerate(self.lv) for slot, (a, b) in enumerate(lv["slots"])),
            key=lambda m: (-far(m), m[0]))
        offs = {(a // lv["h"], b // lv["h"]) for lv in self.lv for a, b in lv["slots"]}
        self.everyone = sorted(offs | {((-a) % nx, (-b) % ny) for a, b in offs}, key=lambda q: (-hops(*q), q))

    def constants(self):
        ch, rows, cols = self.ch, self.rows, self.cols
        q_parts, p_parts = [], []
        for lv in self.lv:
            p, h, ur, uc, nb, nq, qr = (lv[x] for x in ("p", "h", "ur", "uc", "nb", "nq", "qrows"))
            q = np.zeros((h, nb, qr, rows * 8), np.float32)
            for hx in range(h):
                for b in range(nb):
                    for t in range(nq):
                        rho = b * nq + t
                        if rho < ch * ur:
                            c, rr = divmod(rho, ur)
                            for u in range(p):
                                q[hx, b, t, ((hx * ur + rr) * p + u) * 8 + c] = 1.0 / p
            q_parts.append(q.reshape(h * nb * qr, rows * 8))
            for hy in range(h):
                pm = np.zeros((cols, cols), np.float32)
                for j in range(uc):
                    for b in range(nb):
                        pm[(hy * uc + j) * p:(hy * uc + j + 1) * p, b * uc + j] = 1.0 / p
                p_parts.append(pm)
        bf = lambda z: np.asarray(z).astype(jnp.bfloat16)
        out = [bf(np.concatenate(q_parts, 0)), bf(np.concatenate(p_parts, 0))]

        ky = np.arange(MODES_Y)
        mx = np.arange(MODES_X)
        kx = np.where(mx < MODES_X // 2, mx, mx - MODES_X)
        ty = 2 * np.pi * ((np.arange(cols)[None, :] * ky[:, None]) % cols) / cols
        wide = np.concatenate([np.tile(np.cos(ty).T, (1, 2 * MODES_X)), np.tile(np.sin(ty).T, (1, 2 * MODES_X))], 1)
        dh, dl = np_split(wide)
        out.append(np.concatenate([dh, dh, dl], 0))
        tx = 2 * np.pi * ((np.arange(rows)[:, None] * kx[None, :]) % rows) / rows
        cx, sx = np.cos(tx), np.sin(tx)
        cr, sr = np.repeat(cx, MODES_Y, axis=1), np.repeat(sx, MODES_Y, axis=1)
        turns = np.concatenate([cr, -sr, -sr, -cr], 1).astype(np.float32)
        out.append(turns)
        out.append(np.stack([turns[ws].sum(0) for lv in self.lv for _, ws in lv["origin"]]))
        ir = np.zeros((2, MODES_X, MODES_Y, rows, 2, MODES_Y))
        for y in range(MODES_Y):
            ir[0, :, y, :, 0, y] = cx.T
            ir[0, :, y, :, 1, y] = sx.T
            ir[1, :, y, :, 0, y] = -sx.T
            ir[1, :, y, :, 1, y] = cx.T
        ir = ir.reshape(2 * MODES_X * MODES_Y, rows * 2 * MODES_Y)
        ih, il = np_split(ir)
        out.append(np.concatenate([ih, ih, il], 0))
        fold = SCALE * np.where(ky == 0, 1.0, 2.0)[:, None] / (rows * cols)
        inv = np.concatenate([np.cos(ty) * fold, -np.sin(ty) * fold], 0)
        gr = 64 // (2 * MODES_Y)
        bd = np.zeros((gr, 2 * MODES_Y, gr, cols))
        for g in range(gr):
            bd[g, :, g, :] = inv
        bh, bl = np_split(bd.reshape(gr * 2 * MODES_Y, gr * cols))
        out.append(np.concatenate([bh, bh, bl, np.zeros_like(bl)], 0))
        return out


LINEAR = math.sqrt(2.0 / math.pi)
SCALE = (0.044715 * LINEAR) ** (1.0 / 3.0)
SHIFT = LINEAR / SCALE


def scaled_gelu(w):
    return w + w * jnp.tanh(w * (w * w + SHIFT))


def kernel(plan, hid, inn, *refs):
    hbm, out, vm = refs[:19], refs[19], refs[20:39]
    (fields, wbuf, lw, lb, bw, lyb, miw, mib, mow, mob, pw, pb, qm, pm, dft, tw, tab, ir, bd) = vm
    (cur, feat, lwm, lwt, pk1, pk2, u1, u2, u3, r1, r2, r3, lfs, pjs, pbs, wf, win, bcol, wp, lift_b,
     csem, ssem, rsem) = refs[39:]
    lanes = MODES_X * MODES_Y
    ch, rows, cols, nx, ny = plan.ch, plan.rows, plan.cols, plan.nx, plan.ny
    pks, us, recvs = (pk1, pk2, pk2), (u1, u2, u3), (r1, r2, r3)
    ix, iy = lax.axis_index("gx"), lax.axis_index("gy")

    loads = [pltpu.make_async_copy(h, v, csem.at[n]) for n, (h, v) in enumerate(zip(hbm, vm))]
    for n in (0, 12, 13):
        loads[n].start()
    everyone = plan.everyone
    barrier = pltpu.get_barrier_semaphore()
    for a, b in everyone:
        pl.semaphore_signal(barrier, inc=1, device_id=(lax.rem(ix + a, nx), lax.rem(iy + b, ny)),
                            device_id_type=MESH)
    for n in tuple(range(2, 12)) + (1,) + tuple(range(14, 19)):
        loads[n].start()

    cur[...] = jnp.zeros_like(cur)
    sub = lax.broadcasted_iota(jnp.int32, (rows * FP, cols), 0) % FP
    feat[...] = jnp.where(sub == 4 * ch, 1.0, 0.0).astype(F32)
    for u in us:
        u[...] = jnp.zeros_like(u)
    for n in (0, 12, 13):
        loads[n].wait()
    for c in range(ch):
        cur[pl.ds(c, rows, stride=8), :] = fields[c]

    def pool():
        ch_, cl_ = split(cur[...])
        s = bdot(qm[...], ch_) + bdot(qm[...], cl_)
        sh, sl = split(s)
        start, pstart = 0, 0
        for n, lv in enumerate(plan.lv):
            h, nb, qr, uc = lv["h"], lv["nb"], lv["qrows"], lv["uc"]
            size = h * nb * qr
            lane = lax.broadcasted_iota(jnp.int32, (qr, cols), 1) // uc
            for hy in range(h):
                pmk = pm[pstart:pstart + cols, :]
                pstart += cols
                t = bdot(sh[start:start + size], pmk) + bdot(sl[start:start + size], pmk)
                for hx in range(h):
                    v = t[hx * nb * qr:hx * nb * qr + qr]
                    for b in range(1, nb):
                        o = (hx * nb + b) * qr
                        v = jnp.where(lane == b, t[o:o + qr], v)
                    pks[n][hx * h + hy, lv["at"]:lv["at"] + lv["nq"]] = v[0:lv["nq"]]
            start += size

    def send(step):
        for n, slot, a, b in plan.messages:
            lv = plan.lv[n]
            h = lv["h"]
            pltpu.make_async_remote_copy(
                src_ref=pks[n].at[(a % h) * h + b % h, 0:lv["send"]],
                dst_ref=recvs[n].at[step, slot, 0:lv["send"]],
                send_sem=ssem.at[step, n], recv_sem=rsem.at[step, n],
                device_id=(lax.rem(ix - a // h + nx, nx), lax.rem(iy - b // h + ny, ny)),
                device_id_type=MESH).start()

    def wait_level(step, sems, n):
        ref = recvs[n].at[step, :, 0:plan.lv[n]["send"]]
        pltpu.make_async_copy(ref, ref, sems.at[step, n]).wait()

    nf = lw.shape[0]
    hp = functools.partial(jnp.dot, precision=lax.Precision.HIGHEST, preferred_element_type=F32)
    row_of = lambda ref: ref[...].reshape(1, ref.shape[0])
    pool()
    pl.semaphore_wait(barrier, len(everyone))
    send(0)
    for n in range(2, 12):
        loads[n].wait()
    lfs[...] = jnp.zeros_like(lfs)
    lfs[0:nf, :] = lw[...]
    lfs[nf:nf + 1, :] = row_of(lb)
    lf = lfs[...]
    fr = lift_b.shape[0] // 2
    t = jnp.concatenate([jnp.broadcast_to(lf[f:f + 1], (MODES_Y, hid)) for f in range(fr // MODES_Y)], axis=0)
    t = jnp.concatenate([t] * MODES_Y, axis=1)
    rr = lax.broadcasted_iota(jnp.int32, t.shape, 0) % MODES_Y
    ll = lax.broadcasted_iota(jnp.int32, t.shape, 1) // hid
    h, l = split(jnp.where(rr == ll, t, 0.0))
    lift_b[0:fr, :] = h
    lift_b[fr:2 * fr, :] = l
    wb = hp(lf, bw[...])
    wb = wb + jnp.where(lax.broadcasted_iota(jnp.int32, wb.shape, 0) == nf, row_of(lyb), 0.0)
    h, l = split(SCALE * wb.T)
    wf[...] = jnp.concatenate([h, h, l], axis=1)
    pjs[...] = jnp.zeros_like(pjs)
    pjs[0:ch, 0:hid + inn] = jnp.concatenate([pw[...], hp(pw[...], mow[...])], axis=1)
    pj = pjs[:, 0:hid + inn]
    h, l = split((0.5 / SCALE) * pj[:, hid:hid + inn])
    wp[...] = jnp.concatenate(
        [jnp.concatenate([h, h], axis=1), jnp.concatenate([l, jnp.zeros_like(l)], axis=1)], axis=0)
    pbs[...] = jnp.zeros_like(pbs)
    pbs[0:1, 0:inn] = row_of(mib)
    pbs[1:2, 0:ch] = row_of(pb)
    bcol[...] = pbs[...].T
    ob = bcol[0:8, 1:2] + jnp.sum(pj[:, 0:hid] * row_of(mob), axis=1, keepdims=True)
    zero = lambda c: jnp.zeros((8, c), F32)
    h, l = split(jnp.concatenate([0.5 * miw[...].T, (0.5 / SCALE) * pj[:, 0:hid], zero(hid)], axis=0))
    bh, bl = split(jnp.concatenate([SCALE * bcol[0:inn, 0:1], ob, zero(1)], axis=0))
    win[...] = jnp.concatenate([h, h, l, bh, bl, jnp.zeros((inn + 16, 14), BF16)], axis=1)
    def transform(x):
        hi, lo = split(x)
        return bdot(jnp.concatenate([hi, lo, hi], axis=1), dft[...])

    def turn(z, t):
        return z[:, 0:2 * lanes] * t[:, 0:2 * lanes] + z[:, 2 * lanes:4 * lanes] * t[:, 2 * lanes:4 * lanes]

    def add_up(p, owners):
        sums = [None] * ch
        for v in range(0, len(owners), 8):
            own = owners[v:v + 8]
            for c in range(ch):
                at = [i for i in range(8) if own[i] == c]
                if at:
                    q = p[v:v + 8]
                    if any(o not in (None, c) for o in own):
                        assert at == list(range(at[0], at[-1] + 1))
                        i = lax.broadcasted_iota(jnp.int32, q.shape, 0)
                        q = jnp.where((i >= at[0]) & (i <= at[-1]), q, 0.0)
                    sums[c] = q if sums[c] is None else sums[c] + q
        return [jnp.sum(q, axis=0, keepdims=True) for q in sums]

    def mix(hf, at):
        hf = jnp.concatenate(hf, axis=0)
        turned = pltpu.roll(hf, lanes, 1)
        first = lax.broadcasted_iota(jnp.int32, hf.shape, 1) < lanes
        f1, f2 = jnp.where(first, hf, turned), jnp.where(first, turned, -hf)
        return (sum(f1[c:c + 1] * lwt[at + c] for c in range(ch)), sum(f2[c:c + 1] * lwt[at + c] for c in range(ch)))

    for step in range(STEPS):
        if step > 0:
            send(step)
        if step == 0:
            loads[1].wait()
            for m in range(MODES_X):
                w = jnp.concatenate(
                    [wbuf[part, m].reshape(MODES_Y * hid, hid) for part in range(2)], axis=1)
                wh, wl = split(w)
                q = bdot(lift_b[...], jnp.concatenate([wh, wl], axis=1))
                lwm[m] = q[0:fr, 0:2 * hid] + q[fr:, 0:2 * hid] + q[0:fr, 2 * hid:4 * hid]
            for f in range(nf + 1):
                t = lwm[:, f * MODES_Y:(f + 1) * MODES_Y, :].reshape(lanes, 2 * hid).T
                lwt[f] = jnp.concatenate([t[0:hid], t[hid:2 * hid]], axis=1)
            for n in range(14, 19):
                loads[n].wait()
        z = transform(jnp.concatenate([cur[pl.ds(c, rows, stride=8), :] for c in range(ch)], axis=0))
        z = turn(z, jnp.concatenate([tw[...]] * ch, axis=0))
        ga, gb = mix(add_up(z, [c for c in range(ch) for _ in range(rows)]), 0)
        at = lax.broadcasted_iota(jnp.int32, (hid, 2 * lanes), 1) % lanes
        ga = ga + jnp.where(at == 0, float(rows * cols), 0.0) * lwt[nf]
        for r in range(rows):
            feat[r * FP:r * FP + 8, :] = jnp.where(
                lax.broadcasted_iota(jnp.int32, (8, cols), 0) < ch, cur[r * 8:(r + 1) * 8, :],
                feat[r * FP:r * FP + 8, :])
        starts = [sum(len(q["origin"]) for q in plan.lv[:n]) for n in range(len(plan.lv))]
        for n in range(len(plan.lv)):
            lv = plan.lv[n]
            start = starts[n]
            if n == 0:
                wait_level(step, rsem, n)
            elif n == 1:
                for later in range(1, len(plan.lv)):
                    wait_level(step, rsem, later)
            p, h, sr, ur, uc, nq = (lv[x] for x in ("p", "h", "sr", "ur", "uc", "nq"))
            u = us[n]
            for x, a in enumerate(lv["dxs"]):
                for y, b in enumerate(lv["dys"]):
                    own = (a // h, b // h) == (0, 0)
                    m = n if own or (a, b) in lv["index"] else n - 1
                    k = plan.lv[n]["at"]
                    block = (pks[n][a * h + b, k:k + nq] if own
                             else recvs[m][step, plan.lv[m]["index"][a, b], k:k + nq])
                    u[x * sr:x * sr + nq, y * cols:(y + 1) * cols] = block
            groups = []
            kpad, nb, uc, origin = lv["kpad"], lv["nb"], lv["uc"], lv["origin"]
            lane = lax.broadcasted_iota(jnp.int32, (kpad, cols), 1)
            for b in range(len(origin) // kpad):
                for d in range(lv["c0"] // uc, (lv["c0"] + cols - 1) // uc + 1):
                    y = lv["dys"].index(d % (h * ny))
                    block = u[:, y * cols:(y + 1) * cols]
                    shift = ((d - b) * uc - lv["c0"]) % cols
                    block = pltpu.roll(block, shift, 1) if shift else block
                    l0 = d * uc - lv["c0"]
                    acc = block if l0 <= 0 else jnp.where(lane >= l0, block, acc)
                groups.append(acc)
            ctx = jnp.concatenate(groups, axis=0)
            z = turn(transform(ctx), tab[start:start + len(origin), :])
            ma, mb = mix(add_up(z, [c for c, _ in origin]), ch * (n + 1))
            ga, gb = ga + ma, gb + mb
            for i, (c, ws) in enumerate(origin):
                for w in ws:
                    k = w * FP + ch * (n + 1) + c
                    feat[k:k + 1, :] = ctx[i:i + 1]
        fh, fl = split(feat[...])
        gh, gl = split(ga + pltpu.roll(gb, lanes, 1))
        ball = bdot(jnp.concatenate([gh, gl, gh], axis=1), ir[...])
        low = lax.broadcasted_iota(jnp.int32, (hid, 128), 1) < 64
        pieces = []
        for k in range(ball.shape[1] // 128):
            p = ball[:, k * 128:(k + 1) * 128]
            q = pltpu.roll(p, 64, 1)
            for a, b in ((p, q), (q, p)):
                rest = b - b.astype(BF16).astype(F32)
                pieces.append(jnp.concatenate([jnp.where(low, a, rest).astype(BF16), a.astype(BF16)], axis=1))
        q = bdot(jnp.concatenate(pieces, axis=0), bd[...])
        ones = jnp.where(lax.broadcasted_iota(jnp.int32, (16, rows * cols), 0) < 2, 1.0, 0.0).astype(BF16)
        for blk in range(rows // rows):
            r0 = blk * rows
            cat = lambda x: jnp.concatenate(
                [x[(r0 + k) * FP:(r0 + k + 1) * FP] for k in range(rows)], axis=1)
            fhc, flc = cat(fh), cat(fl)
            v = jnp.concatenate([q[j * hid:(j + 1) * hid] for j in range(len(pieces))], axis=1)
            v = v + bdot(wf[...], jnp.concatenate([fhc, flc, fhc], axis=0))
            mh, ml = split(scaled_gelu(v))
            t = bdot(win[...], jnp.concatenate([mh, ml, mh, ones], axis=0))
            ih, il = split(scaled_gelu(t[0:inn]))
            o = bdot(wp[...], jnp.concatenate([ih, il], axis=0))
            ov = o[0:8] + o[8:16] + t[inn:inn + 8]
            for k in range(rows):
                cur[(r0 + k) * 8:(r0 + k + 1) * 8, :] += ov[:, k * cols:(k + 1) * cols]
        for n in range(len(plan.lv)):
            wait_level(step, ssem, n)
        if step < STEPS - 1:
            pool()
    for c in range(ch):
        out[c] = cur[pl.ds(c, rows, stride=8), :]


def shards(plan, fields, lift_weight, lift_bias, spectral_weight, bypass_weight, layer_bias, mlp_in_weight,
           mlp_in_bias, mlp_out_weight, mlp_out_bias, project_weight, project_bias):
    ch, rows, cols = fields.shape
    hid = lift_weight.shape[1]
    inn = mlp_in_weight.shape[1]
    consts = [jnp.asarray(c) for c in plan.constants()]
    args = [fields, spectral_weight, lift_weight, lift_bias, bypass_weight, layer_bias, mlp_in_weight,
            mlp_in_bias, mlp_out_weight.T, mlp_out_bias, project_weight.T, project_bias] + consts
    assert len(args) == 19
    scratch = [pltpu.VMEM(a.shape, a.dtype) for a in args]
    fr = round_up(4 * ch + 1, 2) * MODES_Y
    scratch += [
        pltpu.VMEM((rows * 8, cols), F32),
        pltpu.VMEM((rows * FP, cols), F32),
        pltpu.VMEM((MODES_X, fr, 2 * hid), F32),
        pltpu.VMEM((4 * ch + 1, hid, 2 * MODES_X * MODES_Y), F32),
    ]
    scratch += [pltpu.VMEM((lv["h"] ** 2, 8, cols), F32) for lv in plan.lv[:2]]
    scratch += [pltpu.VMEM((lv["kpad"], len(lv["dys"]) * cols), F32) for lv in plan.lv]
    scratch += [pltpu.VMEM((STEPS, len(lv["slots"]), lv["sr"], cols), F32) for lv in plan.lv]
    wide = round_up(max(inn, cols), 128)
    scratch += [
        pltpu.VMEM((FP, hid), F32),
        pltpu.VMEM((8, round_up(hid + inn, 128)), F32),
        pltpu.VMEM((8, wide), F32),
        pltpu.VMEM((hid, 3 * FP), BF16),
        pltpu.VMEM((inn + 16, 3 * hid + 16), BF16),
        pltpu.VMEM((wide, 8), F32),
        pltpu.VMEM((16, 2 * inn), BF16),
        pltpu.VMEM((2 * fr, MODES_Y * hid), BF16),
    ]
    scratch += [pltpu.SemaphoreType.DMA((len(args),)), pltpu.SemaphoreType.DMA((STEPS, len(plan.lv))),
                pltpu.SemaphoreType.DMA((STEPS, len(plan.lv)))]
    return pl.pallas_call(
        functools.partial(kernel, plan, hid, inn),
        out_shape=pltpu.VMEM(fields.shape, F32),
        in_specs=[pl.BlockSpec(memory_space=pl.ANY)] * len(args),
        out_specs=pl.BlockSpec(memory_space=pltpu.VMEM),
        scratch_shapes=scratch,
        compiler_params=pltpu.CompilerParams(collective_id=0, has_side_effects=True,
                                             vmem_limit_bytes=60 * 1024 * 1024),
    )(*args)


def solution(mesh):
    nx, ny = mesh.shape["gx"], mesh.shape["gy"]

    def body(fields, *rest):
        plan = Plan(*fields.shape, nx, ny)
        return shards(plan, fields, *rest)

    placed = (P(None, "gx", "gy"),) + (P(),) * 11
    return jax.shard_map(body, mesh=mesh, in_specs=placed, out_specs=P(None, "gx", "gy"), check_vma=False)
```

```python
import functools
import math

import jax
import jax.numpy as jnp
import numpy as np
from jax import lax
from jax.experimental import pallas as pl
from jax.experimental.pallas import tpu as pltpu
from jax.sharding import PartitionSpec as P

MODES_X = 8
MODES_Y = 8
STEPS = 2
LEVELS = (1, 2, 3)
F32 = jnp.float32
BF16 = jnp.bfloat16
FP = 16
MESH = pl.DeviceIdType.MESH


def np_split(a):
    a = np.asarray(a, np.float32)
    hi = a.astype(jnp.bfloat16)
    lo = (a - hi.astype(np.float32)).astype(jnp.bfloat16)
    return hi, lo


def split(x):
    hi = x.astype(BF16)
    lo = (x - hi.astype(F32)).astype(BF16)
    return hi, lo


def bdot(a, b):
    return jnp.dot(a, b, preferred_element_type=F32)


def round_up(n, m):
    return -(-n // m) * m


class Plan:
    def __init__(self, ch, rows, cols, nx, ny):
        self.ch, self.rows, self.cols, self.nx, self.ny = ch, rows, cols, nx, ny
        self.lv = []
        for k in LEVELS:
            p = 2**k
            h = 2 if k == 1 else 1
            nr, nc = rows // p, cols // p
            ur, uc = nr // h, nc // h
            nb = cols // uc
            nq = -(-ch * ur // nb)
            slot_rows = nq if nq in (1, 2, 4) else round_up(nq, 8)
            r0, c0 = -(p - 1) * nr // 2, -(p - 1) * nc // 2
            dxs = sorted({d % (h * nx) for d in range(r0 // ur, (r0 + rows - 1) // ur + 1)})
            dys = sorted({d % (h * ny) for d in range(c0 // uc, (c0 + cols - 1) // uc + 1)})
            slots = [(a, b) for a in dxs for b in dys if (a // h, b // h) != (0, 0)]
            kpad = round_up(len(dxs) * slot_rows, 8)
            origin = []
            for b in range(-(-ch * ur // nq)):
                for i in range(kpad):
                    x, t = divmod(i, slot_rows)
                    c, rr = divmod(b * nq + t, ur)
                    ok = x < len(dxs) and t < nq and c < ch
                    ws = [w for w in range(rows) if ok and (w + r0) % ur == rr
                          and (w + r0) // ur % (h * nx) == dxs[x]]
                    origin.append((c, ws) if ok else (None, []))
            self.lv.append(
                dict(p=p, h=h, ur=ur, uc=uc, nb=nb, nq=nq, sr=slot_rows, r0=r0, c0=c0, dxs=dxs, dys=dys,
                     slots=slots, index={q: n for n, q in enumerate(slots)}, kpad=kpad, origin=origin,
                     qrows=round_up(nq, 8))
            )
        one, two, three = self.lv
        assert two["h"] == three["h"] == 1 and two["nq"] + three["nq"] <= 8
        three["slots"] = [q for q in three["slots"] if q not in two["index"]]
        three["index"] = {q: n for n, q in enumerate(three["slots"])}
        one.update(at=0, send=one["nq"])
        two.update(at=three["nq"], send=two["nq"] + three["nq"])
        three.update(at=0, send=three["nq"])

        def hops(a, b):
            mx = max(nx // 2, 1)
            gx = max(abs(i // mx - (i + a) % nx // mx) + abs(i % mx - (i + a) % nx % mx) for i in range(nx))
            gy = max(abs(j // 2 - (j + b) % ny // 2) for j in range(ny))
            return gx + gy

        def far(m):
            h = self.lv[m[0]]["h"]
            return hops((-(m[2] // h)) % nx, (-(m[3] // h)) % ny)

        self.messages = sorted(
            ((n, slot, a, b) for n, lv in enumerate(self.lv) for slot, (a, b) in enumerate(lv["slots"])),
            key=lambda m: (-far(m), m[0]))
        offs = {(a // lv["h"], b // lv["h"]) for lv in self.lv for a, b in lv["slots"]}
        self.everyone = sorted(offs | {((-a) % nx, (-b) % ny) for a, b in offs}, key=lambda q: (-hops(*q), q))

    def constants(self):
        ch, rows, cols = self.ch, self.rows, self.cols
        q_parts, p_parts = [], []
        for lv in self.lv:
            p, h, ur, uc, nb, nq, qr = (lv[x] for x in ("p", "h", "ur", "uc", "nb", "nq", "qrows"))
            q = np.zeros((h, nb, qr, rows * 8), np.float32)
            for hx in range(h):
                for b in range(nb):
                    for t in range(nq):
                        rho = b * nq + t
                        if rho < ch * ur:
                            c, rr = divmod(rho, ur)
                            for u in range(p):
                                q[hx, b, t, ((hx * ur + rr) * p + u) * 8 + c] = 1.0 / p
            q_parts.append(q.reshape(h * nb * qr, rows * 8))
            for hy in range(h):
                pm = np.zeros((cols, cols), np.float32)
                for j in range(uc):
                    for b in range(nb):
                        pm[(hy * uc + j) * p:(hy * uc + j + 1) * p, b * uc + j] = 1.0 / p
                p_parts.append(pm)
        bf = lambda z: np.asarray(z).astype(jnp.bfloat16)
        out = [bf(np.concatenate(q_parts, 0)), bf(np.concatenate(p_parts, 0))]

        ky = np.arange(MODES_Y)
        mx = np.arange(MODES_X)
        kx = np.where(mx < MODES_X // 2, mx, mx - MODES_X)
        ty = 2 * np.pi * ((np.arange(cols)[None, :] * ky[:, None]) % cols) / cols
        wide = np.concatenate([np.tile(np.cos(ty).T, (1, 2 * MODES_X)), np.tile(np.sin(ty).T, (1, 2 * MODES_X))], 1)
        dh, dl = np_split(wide)
        out.append(np.concatenate([dh, dh, dl], 0))
        tx = 2 * np.pi * ((np.arange(rows)[:, None] * kx[None, :]) % rows) / rows
        cx, sx = np.cos(tx), np.sin(tx)
        cr, sr = np.repeat(cx, MODES_Y, axis=1), np.repeat(sx, MODES_Y, axis=1)
        turns = np.concatenate([cr, -sr, -sr, -cr], 1).astype(np.float32)
        out.append(turns)
        out.append(np.stack([turns[ws].sum(0) for lv in self.lv for _, ws in lv["origin"]]))
        ir = np.zeros((2, MODES_X, MODES_Y, rows, 2, MODES_Y))
        for y in range(MODES_Y):
            ir[0, :, y, :, 0, y] = cx.T
            ir[0, :, y, :, 1, y] = sx.T
            ir[1, :, y, :, 0, y] = -sx.T
            ir[1, :, y, :, 1, y] = cx.T
        ir = ir.reshape(2 * MODES_X * MODES_Y, rows * 2 * MODES_Y)
        ih, il = np_split(ir)
        out.append(np.concatenate([ih, ih, il], 0))
        fold = SCALE * np.where(ky == 0, 1.0, 2.0)[:, None] / (rows * cols)
        inv = np.concatenate([np.cos(ty) * fold, -np.sin(ty) * fold], 0)
        gr = 64 // (2 * MODES_Y)
        bd = np.zeros((gr, 2 * MODES_Y, gr, cols))
        for g in range(gr):
            bd[g, :, g, :] = inv
        bh, bl = np_split(bd.reshape(gr * 2 * MODES_Y, gr * cols))
        out.append(np.concatenate([bh, bh, bl, np.zeros_like(bl)], 0))
        return out


LINEAR = math.sqrt(2.0 / math.pi)
SCALE = (0.044715 * LINEAR) ** (1.0 / 3.0)
SHIFT = LINEAR / SCALE


def scaled_gelu(w):
    return w + w * jnp.tanh(w * (w * w + SHIFT))


def kernel(plan, hid, inn, *refs):
    hbm, out, vm = refs[:19], refs[19], refs[20:39]
    (fields, wbuf, lw, lb, bw, lyb, miw, mib, mow, mob, pw, pb, qm, pm, dft, tw, tab, ir, bd) = vm
    (cur, feat, lwm, lwt, pk1, pk2, u1, u2, u3, r1, r2, r3, lfs, pjs, pbs, wf, win, bcol, wp, lift_b,
     csem, ssem, rsem) = refs[39:]
    lanes = MODES_X * MODES_Y
    ch, rows, cols, nx, ny = plan.ch, plan.rows, plan.cols, plan.nx, plan.ny
    pks, us, recvs = (pk1, pk2, pk2), (u1, u2, u3), (r1, r2, r3)
    ix, iy = lax.axis_index("gx"), lax.axis_index("gy")

    loads = [pltpu.make_async_copy(h, v, csem.at[n]) for n, (h, v) in enumerate(zip(hbm, vm))]
    for n in (0, 12, 13):
        loads[n].start()
    everyone = plan.everyone
    barrier = pltpu.get_barrier_semaphore()
    for a, b in everyone:
        pl.semaphore_signal(barrier, inc=1, device_id=(lax.rem(ix + a, nx), lax.rem(iy + b, ny)),
                            device_id_type=MESH)
    for n in tuple(range(2, 12)) + (1,) + tuple(range(14, 19)):
        loads[n].start()

    cur[...] = jnp.zeros_like(cur)
    sub = lax.broadcasted_iota(jnp.int32, (rows * FP, cols), 0) % FP
    feat[...] = jnp.where(sub == 4 * ch, 1.0, 0.0).astype(F32)
    for u in us:
        u[...] = jnp.zeros_like(u)
    for n in (0, 12, 13):
        loads[n].wait()
    for c in range(ch):
        cur[pl.ds(c, rows, stride=8), :] = fields[c]

    def pool():
        ch_, cl_ = split(cur[...])
        s = bdot(qm[...], ch_) + bdot(qm[...], cl_)
        sh, sl = split(s)
        start, pstart = 0, 0
        for n, lv in enumerate(plan.lv):
            h, nb, qr, uc = lv["h"], lv["nb"], lv["qrows"], lv["uc"]
            size = h * nb * qr
            lane = lax.broadcasted_iota(jnp.int32, (qr, cols), 1) // uc
            for hy in range(h):
                pmk = pm[pstart:pstart + cols, :]
                pstart += cols
                t = bdot(sh[start:start + size], pmk) + bdot(sl[start:start + size], pmk)
                for hx in range(h):
                    v = t[hx * nb * qr:hx * nb * qr + qr]
                    for b in range(1, nb):
                        o = (hx * nb + b) * qr
                        v = jnp.where(lane == b, t[o:o + qr], v)
                    pks[n][hx * h + hy, lv["at"]:lv["at"] + lv["nq"]] = v[0:lv["nq"]]
            start += size

    def send(step):
        for n, slot, a, b in plan.messages:
            lv = plan.lv[n]
            h = lv["h"]
            pltpu.make_async_remote_copy(
                src_ref=pks[n].at[(a % h) * h + b % h, 0:lv["send"]],
                dst_ref=recvs[n].at[step, slot, 0:lv["send"]],
                send_sem=ssem.at[step, n], recv_sem=rsem.at[step, n],
                device_id=(lax.rem(ix - a // h + nx, nx), lax.rem(iy - b // h + ny, ny)),
                device_id_type=MESH).start()

    def wait_level(step, sems, n):
        ref = recvs[n].at[step, :, 0:plan.lv[n]["send"]]
        pltpu.make_async_copy(ref, ref, sems.at[step, n]).wait()

    nf = lw.shape[0]
    hp = functools.partial(jnp.dot, precision=lax.Precision.HIGHEST, preferred_element_type=F32)
    row_of = lambda ref: ref[...].reshape(1, ref.shape[0])
    pool()
    pl.semaphore_wait(barrier, len(everyone))
    send(0)
    for n in range(2, 12):
        loads[n].wait()
    lfs[...] = jnp.zeros_like(lfs)
    lfs[0:nf, :] = lw[...]
    lfs[nf:nf + 1, :] = row_of(lb)
    lf = lfs[...]
    fr = lift_b.shape[0] // 2
    t = jnp.concatenate([jnp.broadcast_to(lf[f:f + 1], (MODES_Y, hid)) for f in range(fr // MODES_Y)], axis=0)
    t = jnp.concatenate([t] * MODES_Y, axis=1)
    rr = lax.broadcasted_iota(jnp.int32, t.shape, 0) % MODES_Y
    ll = lax.broadcasted_iota(jnp.int32, t.shape, 1) // hid
    h, l = split(jnp.where(rr == ll, t, 0.0))
    lift_b[0:fr, :] = h
    lift_b[fr:2 * fr, :] = l
    wb = hp(lf, bw[...])
    wb = wb + jnp.where(lax.broadcasted_iota(jnp.int32, wb.shape, 0) == nf, row_of(lyb), 0.0)
    h, l = split(SCALE * wb.T)
    wf[...] = jnp.concatenate([h, h, l], axis=1)
    pjs[...] = jnp.zeros_like(pjs)
    pjs[0:ch, 0:hid + inn] = jnp.concatenate([pw[...], hp(pw[...], mow[...])], axis=1)
    pj = pjs[:, 0:hid + inn]
    h, l = split((0.5 / SCALE) * pj[:, hid:hid + inn])
    wp[...] = jnp.concatenate(
        [jnp.concatenate([h, h], axis=1), jnp.concatenate([l, jnp.zeros_like(l)], axis=1)], axis=0)
    pbs[...] = jnp.zeros_like(pbs)
    pbs[0:1, 0:inn] = row_of(mib)
    pbs[1:2, 0:ch] = row_of(pb)
    bcol[...] = pbs[...].T
    ob = bcol[0:8, 1:2] + jnp.sum(pj[:, 0:hid] * row_of(mob), axis=1, keepdims=True)
    zero = lambda c: jnp.zeros((8, c), F32)
    h, l = split(jnp.concatenate([0.5 * miw[...].T, (0.5 / SCALE) * pj[:, 0:hid], zero(hid)], axis=0))
    bh, bl = split(jnp.concatenate([SCALE * bcol[0:inn, 0:1], ob, zero(1)], axis=0))
    win[...] = jnp.concatenate([h, h, l, bh, bl, jnp.zeros((inn + 16, 14), BF16)], axis=1)
    def transform(x):
        hi, lo = split(x)
        return bdot(jnp.concatenate([hi, lo, hi], axis=1), dft[...])

    def turn(z, t):
        return z[:, 0:2 * lanes] * t[:, 0:2 * lanes] + z[:, 2 * lanes:4 * lanes] * t[:, 2 * lanes:4 * lanes]

    def add_up(p, owners):
        sums = [None] * ch
        for v in range(0, len(owners), 8):
            own = owners[v:v + 8]
            for c in range(ch):
                at = [i for i in range(8) if own[i] == c]
                if at:
                    q = p[v:v + 8]
                    if any(o not in (None, c) for o in own):
                        assert at == list(range(at[0], at[-1] + 1))
                        i = lax.broadcasted_iota(jnp.int32, q.shape, 0)
                        q = jnp.where((i >= at[0]) & (i <= at[-1]), q, 0.0)
                    sums[c] = q if sums[c] is None else sums[c] + q
        return [jnp.sum(q, axis=0, keepdims=True) for q in sums]

    def mix(hf, at):
        hf = jnp.concatenate(hf, axis=0)
        turned = pltpu.roll(hf, lanes, 1)
        first = lax.broadcasted_iota(jnp.int32, hf.shape, 1) < lanes
        f1, f2 = jnp.where(first, hf, turned), jnp.where(first, turned, -hf)
        return (sum(f1[c:c + 1] * lwt[at + c] for c in range(ch)), sum(f2[c:c + 1] * lwt[at + c] for c in range(ch)))

    for step in range(STEPS):
        if step > 0:
            send(step)
        if step == 0:
            loads[1].wait()
            for m in range(MODES_X):
                w = jnp.concatenate(
                    [wbuf[part, m].reshape(MODES_Y * hid, hid) for part in range(2)], axis=1)
                wh, wl = split(w)
                q = bdot(lift_b[...], jnp.concatenate([wh, wl], axis=1))
                lwm[m] = q[0:fr, 0:2 * hid] + q[fr:, 0:2 * hid] + q[0:fr, 2 * hid:4 * hid]
            for f in range(nf + 1):
                t = lwm[:, f * MODES_Y:(f + 1) * MODES_Y, :].reshape(lanes, 2 * hid).T
                lwt[f] = jnp.concatenate([t[0:hid], t[hid:2 * hid]], axis=1)
            for n in range(14, 19):
                loads[n].wait()
        z = transform(jnp.concatenate([cur[pl.ds(c, rows, stride=8), :] for c in range(ch)], axis=0))
        z = turn(z, jnp.concatenate([tw[...]] * ch, axis=0))
        ga, gb = mix(add_up(z, [c for c in range(ch) for _ in range(rows)]), 0)
        at = lax.broadcasted_iota(jnp.int32, (hid, 2 * lanes), 1) % lanes
        ga = ga + jnp.where(at == 0, float(rows * cols), 0.0) * lwt[nf]
        for r in range(rows):
            feat[r * FP:r * FP + 8, :] = jnp.where(
                lax.broadcasted_iota(jnp.int32, (8, cols), 0) < ch, cur[r * 8:(r + 1) * 8, :],
                feat[r * FP:r * FP + 8, :])
        starts = [sum(len(q["origin"]) for q in plan.lv[:n]) for n in range(len(plan.lv))]
        for n in range(len(plan.lv)):
            lv = plan.lv[n]
            start = starts[n]
            if n == 0:
                wait_level(step, rsem, n)
            elif n == 1:
                for later in range(1, len(plan.lv)):
                    wait_level(step, rsem, later)
            p, h, sr, ur, uc, nq = (lv[x] for x in ("p", "h", "sr", "ur", "uc", "nq"))
            u = us[n]
            for x, a in enumerate(lv["dxs"]):
                for y, b in enumerate(lv["dys"]):
                    own = (a // h, b // h) == (0, 0)
                    m = n if own or (a, b) in lv["index"] else n - 1
                    k = plan.lv[n]["at"]
                    block = (pks[n][a * h + b, k:k + nq] if own
                             else recvs[m][step, plan.lv[m]["index"][a, b], k:k + nq])
                    u[x * sr:x * sr + nq, y * cols:(y + 1) * cols] = block
            groups = []
            kpad, nb, uc, origin = lv["kpad"], lv["nb"], lv["uc"], lv["origin"]
            lane = lax.broadcasted_iota(jnp.int32, (kpad, cols), 1)
            for b in range(len(origin) // kpad):
                for d in range(lv["c0"] // uc, (lv["c0"] + cols - 1) // uc + 1):
                    y = lv["dys"].index(d % (h * ny))
                    block = u[:, y * cols:(y + 1) * cols]
                    shift = ((d - b) * uc - lv["c0"]) % cols
                    block = pltpu.roll(block, shift, 1) if shift else block
                    l0 = d * uc - lv["c0"]
                    acc = block if l0 <= 0 else jnp.where(lane >= l0, block, acc)
                groups.append(acc)
            ctx = jnp.concatenate(groups, axis=0)
            z = turn(transform(ctx), tab[start:start + len(origin), :])
            ma, mb = mix(add_up(z, [c for c, _ in origin]), ch * (n + 1))
            ga, gb = ga + ma, gb + mb
            for i, (c, ws) in enumerate(origin):
                for w in ws:
                    k = w * FP + ch * (n + 1) + c
                    feat[k:k + 1, :] = ctx[i:i + 1]
        fh, fl = split(feat[...])
        gh, gl = split(ga + pltpu.roll(gb, lanes, 1))
        ball = bdot(jnp.concatenate([gh, gl, gh], axis=1), ir[...])
        low = lax.broadcasted_iota(jnp.int32, (hid, 128), 1) < 64
        bypass = jnp.concatenate([jnp.zeros((hid, 64), F32), wf[...].astype(F32), jnp.zeros((hid, 64 - 3 * FP), F32)], axis=1)
        pieces = []
        for k in range(ball.shape[1] // 128):
            p = ball[:, k * 128:(k + 1) * 128]
            q = pltpu.roll(p, 64, 1)
            for a, b in ((p, q), (q, p)):
                rest = b - b.astype(BF16).astype(F32)
                pieces.append(jnp.concatenate([jnp.where(low, a, rest).astype(BF16), jnp.where(low, a, bypass).astype(BF16)], axis=1))
        ones = jnp.where(lax.broadcasted_iota(jnp.int32, (16, rows * cols), 0) < 2, 1.0, 0.0).astype(BF16)
        for blk in range(rows // rows):
            r0 = blk * rows
            per = rows // len(pieces)
            cat = lambda x, i: jnp.concatenate([x[k * FP:(k + 1) * FP] for k in range(i * per, (i + 1) * per)], axis=1)
            none = jnp.zeros((64 - 3 * FP, per * cols), BF16)
            v = jnp.concatenate(
                [bdot(p, jnp.concatenate([bd[0:192, :], cat(fh, i), cat(fl, i), cat(fh, i), none], axis=0))
                 for i, p in enumerate(pieces)], axis=1)
            mh, ml = split(scaled_gelu(v))
            t = bdot(win[...], jnp.concatenate([mh, ml, mh, ones], axis=0))
            ih, il = split(scaled_gelu(t[0:inn]))
            o = bdot(wp[...], jnp.concatenate([ih, il], axis=0))
            ov = o[0:8] + o[8:16] + t[inn:inn + 8]
            for k in range(rows):
                cur[(r0 + k) * 8:(r0 + k + 1) * 8, :] += ov[:, k * cols:(k + 1) * cols]
        for n in range(len(plan.lv)):
            wait_level(step, ssem, n)
        if step < STEPS - 1:
            pool()
    for c in range(ch):
        out[c] = cur[pl.ds(c, rows, stride=8), :]


def shards(plan, fields, lift_weight, lift_bias, spectral_weight, bypass_weight, layer_bias, mlp_in_weight,
           mlp_in_bias, mlp_out_weight, mlp_out_bias, project_weight, project_bias):
    ch, rows, cols = fields.shape
    hid = lift_weight.shape[1]
    inn = mlp_in_weight.shape[1]
    consts = [jnp.asarray(c) for c in plan.constants()]
    args = [fields, spectral_weight, lift_weight, lift_bias, bypass_weight, layer_bias, mlp_in_weight,
            mlp_in_bias, mlp_out_weight.T, mlp_out_bias, project_weight.T, project_bias] + consts
    assert len(args) == 19
    scratch = [pltpu.VMEM(a.shape, a.dtype) for a in args]
    fr = round_up(4 * ch + 1, 2) * MODES_Y
    scratch += [
        pltpu.VMEM((rows * 8, cols), F32),
        pltpu.VMEM((rows * FP, cols), F32),
        pltpu.VMEM((MODES_X, fr, 2 * hid), F32),
        pltpu.VMEM((4 * ch + 1, hid, 2 * MODES_X * MODES_Y), F32),
    ]
    scratch += [pltpu.VMEM((lv["h"] ** 2, 8, cols), F32) for lv in plan.lv[:2]]
    scratch += [pltpu.VMEM((lv["kpad"], len(lv["dys"]) * cols), F32) for lv in plan.lv]
    scratch += [pltpu.VMEM((STEPS, len(lv["slots"]), lv["sr"], cols), F32) for lv in plan.lv]
    wide = round_up(max(inn, cols), 128)
    scratch += [
        pltpu.VMEM((FP, hid), F32),
        pltpu.VMEM((8, round_up(hid + inn, 128)), F32),
        pltpu.VMEM((8, wide), F32),
        pltpu.VMEM((hid, 3 * FP), BF16),
        pltpu.VMEM((inn + 16, 3 * hid + 16), BF16),
        pltpu.VMEM((wide, 8), F32),
        pltpu.VMEM((16, 2 * inn), BF16),
        pltpu.VMEM((2 * fr, MODES_Y * hid), BF16),
    ]
    scratch += [pltpu.SemaphoreType.DMA((len(args),)), pltpu.SemaphoreType.DMA((STEPS, len(plan.lv))),
                pltpu.SemaphoreType.DMA((STEPS, len(plan.lv)))]
    return pl.pallas_call(
        functools.partial(kernel, plan, hid, inn),
        out_shape=pltpu.VMEM(fields.shape, F32),
        in_specs=[pl.BlockSpec(memory_space=pl.ANY)] * len(args),
        out_specs=pl.BlockSpec(memory_space=pltpu.VMEM),
        scratch_shapes=scratch,
        compiler_params=pltpu.CompilerParams(collective_id=0, has_side_effects=True,
                                             vmem_limit_bytes=60 * 1024 * 1024),
    )(*args)


def solution(mesh):
    nx, ny = mesh.shape["gx"], mesh.shape["gy"]

    def body(fields, *rest):
        plan = Plan(*fields.shape, nx, ny)
        return shards(plan, fields, *rest)

    placed = (P(None, "gx", "gy"),) + (P(),) * 11
    return jax.shard_map(body, mesh=mesh, in_specs=placed, out_specs=P(None, "gx", "gy"), check_vma=False)
```

```python
import functools
import math

import jax
import jax.numpy as jnp
import numpy as np
from jax import lax
from jax.experimental import pallas as pl
from jax.experimental.pallas import tpu as pltpu
from jax.sharding import PartitionSpec as P

MODES_X = 8
MODES_Y = 8
STEPS = 2
LEVELS = (1, 2, 3)
F32 = jnp.float32
BF16 = jnp.bfloat16
FP = 16
MESH = pl.DeviceIdType.MESH


def np_split(a):
    a = np.asarray(a, np.float32)
    hi = a.astype(jnp.bfloat16)
    lo = (a - hi.astype(np.float32)).astype(jnp.bfloat16)
    return hi, lo


def split(x):
    hi = x.astype(BF16)
    lo = (x - hi.astype(F32)).astype(BF16)
    return hi, lo


def bdot(a, b):
    return jnp.dot(a, b, preferred_element_type=F32)


def round_up(n, m):
    return -(-n // m) * m


class Plan:
    def __init__(self, ch, rows, cols, nx, ny):
        self.ch, self.rows, self.cols, self.nx, self.ny = ch, rows, cols, nx, ny
        self.lv = []
        for k in LEVELS:
            p = 2**k
            h = 2 if k == 1 else 1
            nr, nc = rows // p, cols // p
            ur, uc = nr // h, nc // h
            nb = cols // uc
            nq = -(-ch * ur // nb)
            slot_rows = nq if nq in (1, 2, 4) else round_up(nq, 8)
            r0, c0 = -(p - 1) * nr // 2, -(p - 1) * nc // 2
            dxs = sorted({d % (h * nx) for d in range(r0 // ur, (r0 + rows - 1) // ur + 1)})
            dys = sorted({d % (h * ny) for d in range(c0 // uc, (c0 + cols - 1) // uc + 1)})
            slots = [(a, b) for a in dxs for b in dys if (a // h, b // h) != (0, 0)]
            kpad = round_up(len(dxs) * slot_rows, 8)
            origin = []
            for b in range(-(-ch * ur // nq)):
                for i in range(kpad):
                    x, t = divmod(i, slot_rows)
                    c, rr = divmod(b * nq + t, ur)
                    ok = x < len(dxs) and t < nq and c < ch
                    ws = [w for w in range(rows) if ok and (w + r0) % ur == rr
                          and (w + r0) // ur % (h * nx) == dxs[x]]
                    origin.append((c, ws) if ok else (None, []))
            self.lv.append(
                dict(p=p, h=h, ur=ur, uc=uc, nb=nb, nq=nq, sr=slot_rows, r0=r0, c0=c0, dxs=dxs, dys=dys,
                     slots=slots, index={q: n for n, q in enumerate(slots)}, kpad=kpad, origin=origin,
                     qrows=round_up(nq, 8))
            )
        one, two, three = self.lv
        assert two["h"] == three["h"] == 1 and two["nq"] + three["nq"] <= 8
        three["slots"] = [q for q in three["slots"] if q not in two["index"]]
        three["index"] = {q: n for n, q in enumerate(three["slots"])}
        one.update(at=0, send=one["nq"])
        two.update(at=three["nq"], send=two["nq"] + three["nq"])
        three.update(at=0, send=three["nq"])

        def hops(a, b):
            mx = max(nx // 2, 1)
            gx = max(abs(i // mx - (i + a) % nx // mx) + abs(i % mx - (i + a) % nx % mx) for i in range(nx))
            gy = max(abs(j // 2 - (j + b) % ny // 2) for j in range(ny))
            return gx + gy

        def far(m):
            h = self.lv[m[0]]["h"]
            return hops((-(m[2] // h)) % nx, (-(m[3] // h)) % ny)

        self.messages = sorted(
            ((n, slot, a, b) for n, lv in enumerate(self.lv) for slot, (a, b) in enumerate(lv["slots"])),
            key=lambda m: (-far(m), m[0]))
        offs = {(a // lv["h"], b // lv["h"]) for lv in self.lv for a, b in lv["slots"]}
        self.everyone = sorted(offs | {((-a) % nx, (-b) % ny) for a, b in offs}, key=lambda q: (-hops(*q), q))

    def constants(self):
        ch, rows, cols = self.ch, self.rows, self.cols
        q_parts, p_parts = [], []
        for lv in self.lv:
            p, h, ur, uc, nb, nq, qr = (lv[x] for x in ("p", "h", "ur", "uc", "nb", "nq", "qrows"))
            q = np.zeros((h, nb, qr, rows * 8), np.float32)
            for hx in range(h):
                for b in range(nb):
                    for t in range(nq):
                        rho = b * nq + t
                        if rho < ch * ur:
                            c, rr = divmod(rho, ur)
                            for u in range(p):
                                q[hx, b, t, ((hx * ur + rr) * p + u) * 8 + c] = 1.0 / p
            q_parts.append(q.reshape(h * nb * qr, rows * 8))
            for hy in range(h):
                pm = np.zeros((cols, cols), np.float32)
                for j in range(uc):
                    for b in range(nb):
                        pm[(hy * uc + j) * p:(hy * uc + j + 1) * p, b * uc + j] = 1.0 / p
                p_parts.append(pm)
        bf = lambda z: np.asarray(z).astype(jnp.bfloat16)
        out = [bf(np.concatenate(q_parts, 0)), bf(np.concatenate(p_parts, 0))]

        ky = np.arange(MODES_Y)
        mx = np.arange(MODES_X)
        kx = np.where(mx < MODES_X // 2, mx, mx - MODES_X)
        ty = 2 * np.pi * ((np.arange(cols)[None, :] * ky[:, None]) % cols) / cols
        wide = np.concatenate([np.tile(np.cos(ty).T, (1, 2 * MODES_X)), np.tile(np.sin(ty).T, (1, 2 * MODES_X))], 1)
        dh, dl = np_split(wide)
        out.append(np.concatenate([dh, dh, dl], 0))
        tx = 2 * np.pi * ((np.arange(rows)[:, None] * kx[None, :]) % rows) / rows
        cx, sx = np.cos(tx), np.sin(tx)
        cr, sr = np.repeat(cx, MODES_Y, axis=1), np.repeat(sx, MODES_Y, axis=1)
        turns = np.concatenate([cr, -sr, -sr, -cr], 1).astype(np.float32)
        out.append(turns)
        out.append(np.stack([turns[ws].sum(0) for lv in self.lv for _, ws in lv["origin"]]))
        ir = np.zeros((2, MODES_X, MODES_Y, rows, 2, MODES_Y))
        for y in range(MODES_Y):
            ir[0, :, y, :, 0, y] = cx.T
            ir[0, :, y, :, 1, y] = sx.T
            ir[1, :, y, :, 0, y] = -sx.T
            ir[1, :, y, :, 1, y] = cx.T
        ir = ir.reshape(2 * MODES_X * MODES_Y, rows * 2 * MODES_Y)
        ih, il = np_split(ir)
        out.append(np.concatenate([ih, ih, il], 0))
        fold = SCALE * np.where(ky == 0, 1.0, 2.0)[:, None] / (rows * cols)
        inv = np.concatenate([np.cos(ty) * fold, -np.sin(ty) * fold], 0)
        gr = 64 // (2 * MODES_Y)
        bd = np.zeros((gr, 2 * MODES_Y, gr, cols))
        for g in range(gr):
            bd[g, :, g, :] = inv
        bh, bl = np_split(bd.reshape(gr * 2 * MODES_Y, gr * cols))
        out.append(np.concatenate([bh, bh, bl, np.zeros_like(bl)], 0))
        return out


LINEAR = math.sqrt(2.0 / math.pi)
SCALE = (0.044715 * LINEAR) ** (1.0 / 3.0)
SHIFT = LINEAR / SCALE


def scaled_gelu(w):
    return w + w * jnp.tanh(w * (w * w + SHIFT))


def kernel(plan, hid, inn, *refs):
    hbm, out, vm = refs[:19], refs[19], refs[20:39]
    (fields, wbuf, lw, lb, bw, lyb, miw, mib, mow, mob, pw, pb, qm, pm, dft, tw, tab, ir, bd) = vm
    (cur, feat, lwm, lwt, pk1, pk2, u1, u2, u3, r1, r2, r3, lfs, pjs, pbs, wf, win, bcol, wp, lift_b,
     csem, ssem, rsem) = refs[39:]
    lanes = MODES_X * MODES_Y
    ch, rows, cols, nx, ny = plan.ch, plan.rows, plan.cols, plan.nx, plan.ny
    pks, us, recvs = (pk1, pk2, pk2), (u1, u2, u3), (r1, r2, r3)
    ix, iy = lax.axis_index("gx"), lax.axis_index("gy")

    loads = [pltpu.make_async_copy(h, v, csem.at[n]) for n, (h, v) in enumerate(zip(hbm, vm))]
    for n in (0, 12, 13):
        loads[n].start()
    everyone = plan.everyone
    barrier = pltpu.get_barrier_semaphore()
    for a, b in everyone:
        pl.semaphore_signal(barrier, inc=1, device_id=(lax.rem(ix + a, nx), lax.rem(iy + b, ny)),
                            device_id_type=MESH)
    for n in tuple(range(2, 12)) + (1,) + tuple(range(14, 19)):
        loads[n].start()

    cur[...] = jnp.zeros_like(cur)
    sub = lax.broadcasted_iota(jnp.int32, (rows * FP, cols), 0) % FP
    feat[...] = jnp.where(sub == 4 * ch, 1.0, 0.0).astype(F32)
    for u in us:
        u[...] = jnp.zeros_like(u)
    for n in (0, 12, 13):
        loads[n].wait()
    for c in range(ch):
        cur[pl.ds(c, rows, stride=8), :] = fields[c]

    def pool():
        ch_, cl_ = split(cur[...])
        s = bdot(qm[...], ch_) + bdot(qm[...], cl_)
        sh, sl = split(s)
        start, pstart = 0, 0
        for n, lv in enumerate(plan.lv):
            h, nb, qr, uc = lv["h"], lv["nb"], lv["qrows"], lv["uc"]
            size = h * nb * qr
            lane = lax.broadcasted_iota(jnp.int32, (qr, cols), 1) // uc
            for hy in range(h):
                pmk = pm[pstart:pstart + cols, :]
                pstart += cols
                t = bdot(sh[start:start + size], pmk) + bdot(sl[start:start + size], pmk)
                for hx in range(h):
                    v = t[hx * nb * qr:hx * nb * qr + qr]
                    for b in range(1, nb):
                        o = (hx * nb + b) * qr
                        v = jnp.where(lane == b, t[o:o + qr], v)
                    pks[n][hx * h + hy, lv["at"]:lv["at"] + lv["nq"]] = v[0:lv["nq"]]
            start += size

    def send(step):
        for n, slot, a, b in plan.messages:
            lv = plan.lv[n]
            h = lv["h"]
            pltpu.make_async_remote_copy(
                src_ref=pks[n].at[(a % h) * h + b % h, 0:lv["send"]],
                dst_ref=recvs[n].at[step, slot, 0:lv["send"]],
                send_sem=ssem.at[step, n], recv_sem=rsem.at[step, n],
                device_id=(lax.rem(ix - a // h + nx, nx), lax.rem(iy - b // h + ny, ny)),
                device_id_type=MESH).start()

    def wait_level(step, sems, n):
        ref = recvs[n].at[step, :, 0:plan.lv[n]["send"]]
        pltpu.make_async_copy(ref, ref, sems.at[step, n]).wait()

    nf = lw.shape[0]
    hp = functools.partial(jnp.dot, precision=lax.Precision.HIGHEST, preferred_element_type=F32)
    row_of = lambda ref: ref[...].reshape(1, ref.shape[0])
    pool()
    pl.semaphore_wait(barrier, len(everyone))
    send(0)
    for n in range(2, 12):
        loads[n].wait()
    lfs[...] = jnp.zeros_like(lfs)
    lfs[0:nf, :] = lw[...]
    lfs[nf:nf + 1, :] = row_of(lb)
    lf = lfs[...]
    fr = lift_b.shape[0] // 2
    t = jnp.concatenate([jnp.broadcast_to(lf[f:f + 1], (MODES_Y, hid)) for f in range(fr // MODES_Y)], axis=0)
    t = jnp.concatenate([t] * MODES_Y, axis=1)
    rr = lax.broadcasted_iota(jnp.int32, t.shape, 0) % MODES_Y
    ll = lax.broadcasted_iota(jnp.int32, t.shape, 1) // hid
    h, l = split(jnp.where(rr == ll, t, 0.0))
    lift_b[0:fr, :] = h
    lift_b[fr:2 * fr, :] = l
    wb = hp(lf, bw[...])
    wb = wb + jnp.where(lax.broadcasted_iota(jnp.int32, wb.shape, 0) == nf, row_of(lyb), 0.0)
    h, l = split(SCALE * wb.T)
    wf[...] = jnp.concatenate([h, h, l], axis=1)
    pjs[...] = jnp.zeros_like(pjs)
    pjs[0:ch, 0:hid + inn] = jnp.concatenate([pw[...], hp(pw[...], mow[...])], axis=1)
    pj = pjs[:, 0:hid + inn]
    h, l = split((0.5 / SCALE) * pj[:, hid:hid + inn])
    wp[...] = jnp.concatenate(
        [jnp.concatenate([h, h], axis=1), jnp.concatenate([l, jnp.zeros_like(l)], axis=1)], axis=0)
    pbs[...] = jnp.zeros_like(pbs)
    pbs[0:1, 0:inn] = row_of(mib)
    pbs[1:2, 0:ch] = row_of(pb)
    bcol[...] = pbs[...].T
    ob = bcol[0:8, 1:2] + jnp.sum(pj[:, 0:hid] * row_of(mob), axis=1, keepdims=True)
    zero = lambda c: jnp.zeros((8, c), F32)
    h, l = split(jnp.concatenate([0.5 * miw[...].T, (0.5 / SCALE) * pj[:, 0:hid], zero(hid)], axis=0))
    bh, bl = split(jnp.concatenate([SCALE * bcol[0:inn, 0:1], ob, zero(1)], axis=0))
    win[...] = jnp.concatenate([h, h, l, bh, bl, jnp.zeros((inn + 16, 14), BF16)], axis=1)
    def transform(x):
        hi, lo = split(x)
        return bdot(jnp.concatenate([hi, lo, hi], axis=1), dft[...])

    def turn(z, t):
        return z[:, 0:2 * lanes] * t[:, 0:2 * lanes] + z[:, 2 * lanes:4 * lanes] * t[:, 2 * lanes:4 * lanes]

    def add_up(p, owners):
        sums = [None] * ch
        for v in range(0, len(owners), 8):
            own = owners[v:v + 8]
            for c in range(ch):
                at = [i for i in range(8) if own[i] == c]
                if at:
                    q = p[v:v + 8]
                    if any(o not in (None, c) for o in own):
                        assert at == list(range(at[0], at[-1] + 1))
                        i = lax.broadcasted_iota(jnp.int32, q.shape, 0)
                        q = jnp.where((i >= at[0]) & (i <= at[-1]), q, 0.0)
                    sums[c] = q if sums[c] is None else sums[c] + q
        return [jnp.sum(q, axis=0, keepdims=True) for q in sums]

    def mix(hf, at):
        hf = jnp.concatenate(hf, axis=0)
        turned = pltpu.roll(hf, lanes, 1)
        first = lax.broadcasted_iota(jnp.int32, hf.shape, 1) < lanes
        f1, f2 = jnp.where(first, hf, turned), jnp.where(first, turned, -hf)
        return (sum(f1[c:c + 1] * lwt[at + c] for c in range(ch)), sum(f2[c:c + 1] * lwt[at + c] for c in range(ch)))

    for step in range(STEPS):
        if step > 0:
            send(step)
        if step == 0:
            loads[1].wait()
            for m in range(MODES_X):
                w = jnp.concatenate(
                    [wbuf[part, m].reshape(MODES_Y * hid, hid) for part in range(2)], axis=1)
                wh, wl = split(w)
                q = bdot(lift_b[...], jnp.concatenate([wh, wl], axis=1))
                lwm[m] = q[0:fr, 0:2 * hid] + q[fr:, 0:2 * hid] + q[0:fr, 2 * hid:4 * hid]
            for f in range(nf + 1):
                t = lwm[:, f * MODES_Y:(f + 1) * MODES_Y, :].reshape(lanes, 2 * hid).T
                lwt[f] = jnp.concatenate([t[0:hid], t[hid:2 * hid]], axis=1)
            for n in range(14, 19):
                loads[n].wait()
        z = transform(jnp.concatenate([cur[pl.ds(c, rows, stride=8), :] for c in range(ch)], axis=0))
        z = turn(z, jnp.concatenate([tw[...]] * ch, axis=0))
        ga, gb = mix(add_up(z, [c for c in range(ch) for _ in range(rows)]), 0)
        at = lax.broadcasted_iota(jnp.int32, (hid, 2 * lanes), 1) % lanes
        ga = ga + jnp.where(at == 0, float(rows * cols), 0.0) * lwt[nf]
        for r in range(rows):
            feat[r * FP:r * FP + 8, :] = jnp.where(
                lax.broadcasted_iota(jnp.int32, (8, cols), 0) < ch, cur[r * 8:(r + 1) * 8, :],
                feat[r * FP:r * FP + 8, :])
        starts = [sum(len(q["origin"]) for q in plan.lv[:n]) for n in range(len(plan.lv))]
        held = []
        for n in range(len(plan.lv)):
            lv = plan.lv[n]
            start = starts[n]
            if n == 0:
                wait_level(step, rsem, n)
            elif n == 1:
                for later in range(1, len(plan.lv)):
                    wait_level(step, rsem, later)
            p, h, sr, ur, uc, nq = (lv[x] for x in ("p", "h", "sr", "ur", "uc", "nq"))
            u = us[n]
            for x, a in enumerate(lv["dxs"]):
                for y, b in enumerate(lv["dys"]):
                    own = (a // h, b // h) == (0, 0)
                    m = n if own or (a, b) in lv["index"] else n - 1
                    k = plan.lv[n]["at"]
                    block = (pks[n][a * h + b, k:k + nq] if own
                             else recvs[m][step, plan.lv[m]["index"][a, b], k:k + nq])
                    u[x * sr:x * sr + nq, y * cols:(y + 1) * cols] = block
            groups = []
            kpad, nb, uc, origin = lv["kpad"], lv["nb"], lv["uc"], lv["origin"]
            lane = lax.broadcasted_iota(jnp.int32, (kpad, cols), 1)
            for b in range(len(origin) // kpad):
                for d in range(lv["c0"] // uc, (lv["c0"] + cols - 1) // uc + 1):
                    y = lv["dys"].index(d % (h * ny))
                    block = u[:, y * cols:(y + 1) * cols]
                    shift = ((d - b) * uc - lv["c0"]) % cols
                    block = pltpu.roll(block, shift, 1) if shift else block
                    l0 = d * uc - lv["c0"]
                    acc = block if l0 <= 0 else jnp.where(lane >= l0, block, acc)
                groups.append(acc)
            ctx = jnp.concatenate(groups, axis=0)
            held.append((n, ctx, start))
            if n != 1:
                z = transform(jnp.concatenate([q for _, q, _ in held], axis=0))
                z = turn(z, tab[held[0][2]:start + len(origin), :])
                for m, _, first in held:
                    own = [c for c, _ in plan.lv[m]["origin"]]
                    at = first - held[0][2]
                    ma, mb = mix(add_up(z[at:at + len(own)], own), ch * (m + 1))
                    ga, gb = ga + ma, gb + mb
                held = []
            for i, (c, ws) in enumerate(origin):
                for w in ws:
                    k = w * FP + ch * (n + 1) + c
                    feat[k:k + 1, :] = ctx[i:i + 1]
        fh, fl = split(feat[...])
        gh, gl = split(ga + pltpu.roll(gb, lanes, 1))
        ball = bdot(jnp.concatenate([gh, gl, gh], axis=1), ir[...])
        low = lax.broadcasted_iota(jnp.int32, (hid, 128), 1) < 64
        bypass = jnp.concatenate([jnp.zeros((hid, 64), F32), wf[...].astype(F32), jnp.zeros((hid, 64 - 3 * FP), F32)], axis=1)
        pieces = []
        for k in range(ball.shape[1] // 128):
            p = ball[:, k * 128:(k + 1) * 128]
            q = pltpu.roll(p, 64, 1)
            for a, b in ((p, q), (q, p)):
                rest = b - b.astype(BF16).astype(F32)
                pieces.append(jnp.concatenate([jnp.where(low, a, rest).astype(BF16), jnp.where(low, a, bypass).astype(BF16)], axis=1))
        ones = jnp.where(lax.broadcasted_iota(jnp.int32, (16, rows * cols), 0) < 2, 1.0, 0.0).astype(BF16)
        for blk in range(rows // rows):
            r0 = blk * rows
            per = rows // len(pieces)
            cat = lambda x, i: jnp.concatenate([x[k * FP:(k + 1) * FP] for k in range(i * per, (i + 1) * per)], axis=1)
            none = jnp.zeros((64 - 3 * FP, per * cols), BF16)
            v = jnp.concatenate(
                [bdot(p, jnp.concatenate([bd[0:192, :], cat(fh, i), cat(fl, i), cat(fh, i), none], axis=0))
                 for i, p in enumerate(pieces)], axis=1)
            mh, ml = split(scaled_gelu(v))
            t = bdot(win[...], jnp.concatenate([mh, ml, mh, ones], axis=0))
            ih, il = split(scaled_gelu(t[0:inn]))
            o = bdot(wp[...], jnp.concatenate([ih, il], axis=0))
            ov = o[0:8] + o[8:16] + t[inn:inn + 8]
            for k in range(rows):
                cur[(r0 + k) * 8:(r0 + k + 1) * 8, :] += ov[:, k * cols:(k + 1) * cols]
        for n in range(len(plan.lv)):
            wait_level(step, ssem, n)
        if step < STEPS - 1:
            pool()
    for c in range(ch):
        out[c] = cur[pl.ds(c, rows, stride=8), :]


def shards(plan, fields, lift_weight, lift_bias, spectral_weight, bypass_weight, layer_bias, mlp_in_weight,
           mlp_in_bias, mlp_out_weight, mlp_out_bias, project_weight, project_bias):
    ch, rows, cols = fields.shape
    hid = lift_weight.shape[1]
    inn = mlp_in_weight.shape[1]
    consts = [jnp.asarray(c) for c in plan.constants()]
    args = [fields, spectral_weight, lift_weight, lift_bias, bypass_weight, layer_bias, mlp_in_weight,
            mlp_in_bias, mlp_out_weight.T, mlp_out_bias, project_weight.T, project_bias] + consts
    assert len(args) == 19
    scratch = [pltpu.VMEM(a.shape, a.dtype) for a in args]
    fr = round_up(4 * ch + 1, 2) * MODES_Y
    scratch += [
        pltpu.VMEM((rows * 8, cols), F32),
        pltpu.VMEM((rows * FP, cols), F32),
        pltpu.VMEM((MODES_X, fr, 2 * hid), F32),
        pltpu.VMEM((4 * ch + 1, hid, 2 * MODES_X * MODES_Y), F32),
    ]
    scratch += [pltpu.VMEM((lv["h"] ** 2, 8, cols), F32) for lv in plan.lv[:2]]
    scratch += [pltpu.VMEM((lv["kpad"], len(lv["dys"]) * cols), F32) for lv in plan.lv]
    scratch += [pltpu.VMEM((STEPS, len(lv["slots"]), lv["sr"], cols), F32) for lv in plan.lv]
    wide = round_up(max(inn, cols), 128)
    scratch += [
        pltpu.VMEM((FP, hid), F32),
        pltpu.VMEM((8, round_up(hid + inn, 128)), F32),
        pltpu.VMEM((8, wide), F32),
        pltpu.VMEM((hid, 3 * FP), BF16),
        pltpu.VMEM((inn + 16, 3 * hid + 16), BF16),
        pltpu.VMEM((wide, 8), F32),
        pltpu.VMEM((16, 2 * inn), BF16),
        pltpu.VMEM((2 * fr, MODES_Y * hid), BF16),
    ]
    scratch += [pltpu.SemaphoreType.DMA((len(args),)), pltpu.SemaphoreType.DMA((STEPS, len(plan.lv))),
                pltpu.SemaphoreType.DMA((STEPS, len(plan.lv)))]
    return pl.pallas_call(
        functools.partial(kernel, plan, hid, inn),
        out_shape=pltpu.VMEM(fields.shape, F32),
        in_specs=[pl.BlockSpec(memory_space=pl.ANY)] * len(args),
        out_specs=pl.BlockSpec(memory_space=pltpu.VMEM),
        scratch_shapes=scratch,
        compiler_params=pltpu.CompilerParams(collective_id=0, has_side_effects=True,
                                             vmem_limit_bytes=60 * 1024 * 1024),
    )(*args)


def solution(mesh):
    nx, ny = mesh.shape["gx"], mesh.shape["gy"]

    def body(fields, *rest):
        plan = Plan(*fields.shape, nx, ny)
        return shards(plan, fields, *rest)

    placed = (P(None, "gx", "gy"),) + (P(),) * 11
    return jax.shard_map(body, mesh=mesh, in_specs=placed, out_specs=P(None, "gx", "gy"), check_vma=False)
```
